512 devices in a mesh: vintage: 16 (over y, core), inline: 4 (over z_hi), xline: 8 (over z_lo, x).
Axes of the slice: x: 4, y: 8, z: 8 (z_hi: 4, z_lo: 2; z = z_hi * 2 + z_lo), core: 2. Of those that a mesh axis runs over, the one named last changes fastest.
Arguments:
- amplitude: float32 [16, 32, 128, 256], P('vintage', 'inline', 'xline'), may hold values from -6 to 6
- inline_slope: int32 [16, 32, 128], P('vintage', 'inline', 'xline'), may hold values from -2 to 2
- crossline_slope: int32 [16, 32, 128], P('vintage', 'inline', 'xline'), may hold values from -2 to 2
Outputs:
- semblance: float32 [16, 32, 128, 256], P('vintage', 'inline', 'xline')
- lag_correl: float32 [16, 32, 128, 264], P('vintage', 'inline', 'xline')
The draws below stay inside these ranges and needn't reach their ends.
All inputs are finite; a program needn't handle non-finite values.
Results may differ from the reference program's by a relative error of at most 0.0003.
Values sent between devices are 32-bit elements; how exact they have to be, the bound alone decides.
No kernel may reach another device: no remote copies, remote signals or barrier semaphores. Data moves between devices by JAX's collectives and lax.ppermute only.
A program may use at most 64 MiB of HBM per device.

```python
import jax
import jax.numpy as jnp
from jax import lax

TIME_SAMPLES = 256
MAX_DIP_STEP = 2
RT = 4
LAGS = 33
NWIN = 8
SURVEY_COUNT = 16
INLINE_TRACES = 32
CROSSLINE_COUNT = 128


def touch_ends(drawn, own_key, smallest, high):
    place = [jax.random.randint(jax.random.fold_in(own_key, axis), (), 0, length) for axis, length in enumerate(drawn.shape)]
    longest = drawn.shape.index(max(drawn.shape))
    beside = place[:longest] + [(place[longest] + 1) % drawn.shape[longest]] + place[longest + 1:]
    return drawn.at[tuple(place)].set(smallest).at[tuple(beside)].set(high)


def block_scale(own_key, shape, split, least, largest):
    def one(dim, shards_of):
        steps = jax.random.uniform(jax.random.fold_in(jax.random.fold_in(own_key, 6), dim), (shards_of,), jnp.float32, least / len(split), largest / len(split))
        return jnp.repeat(jnp.exp(steps), shape[dim] // shards_of).reshape((-1,) + (1,) * (len(shape) - dim - 1))

    level = one(*split[0])
    for cut in split[1:]:
        level = level * one(*cut)
    return level


def centred(rng, shape, width, most, shards=(), kind=jnp.bfloat16):
    array = jax.random.normal(rng, shape, jnp.float32) * width
    if len(shards) > 0:
        array = block_scale(rng, shape, shards, -0.22, 0.18) * array
    return jnp.clip(array, min=-most, max=most).astype(kind)


def setup_inputs(seed: int = 0) -> dict:
    key_of = jax.random.split(jax.random.key(seed), 4)
    return {
        "amplitude": centred(key_of[0], (SURVEY_COUNT, INLINE_TRACES, CROSSLINE_COUNT, TIME_SAMPLES), 1.0, 6.0, ((0, 16), (1, 4), (2, 8)), jnp.float32),
        "inline_slope": touch_ends(jax.random.randint(key_of[1], (SURVEY_COUNT, INLINE_TRACES, CROSSLINE_COUNT), 0 - MAX_DIP_STEP, MAX_DIP_STEP + 1), jax.random.fold_in(key_of[1], 1), 0 - MAX_DIP_STEP, MAX_DIP_STEP).astype(jnp.int32),
        "crossline_slope": touch_ends(jax.random.randint(key_of[2], (SURVEY_COUNT, INLINE_TRACES, CROSSLINE_COUNT), 0 - MAX_DIP_STEP, MAX_DIP_STEP + 1), jax.random.fold_in(key_of[2], 1), 0 - MAX_DIP_STEP, MAX_DIP_STEP).astype(jnp.int32),
    }


EPS = 1e-06

def attribute_padded(padded, dip_il, dip_xl):
    inner_i = padded.shape[0] - 2
    inner_x = padded.shape[1] - 2
    padding = 2 * MAX_DIP_STEP + RT
    extent = TIME_SAMPLES + 2 * RT
    stack = jnp.zeros((inner_i, inner_x, extent), jnp.float32)
    power = jnp.zeros((inner_i, inner_x, extent), jnp.float32)
    for row_step in (-1, 0, 1):
        for col_step in (-1, 0, 1):
            neighbor = padded[1 + row_step:1 + row_step + inner_i, 1 + col_step:1 + col_step + inner_x, :]
            shift_map = row_step * dip_il + col_step * dip_xl
            reach = (abs(row_step) + abs(col_step)) * MAX_DIP_STEP
            moved = jnp.zeros((inner_i, inner_x, extent), jnp.float32)
            for offset_value in range(-reach, reach + 1):
                start = padding - RT + offset_value
                shifted = neighbor[:, :, start:start + extent]
                moved = jnp.where((shift_map == offset_value)[:, :, None], shifted, moved)
            stack = stack + moved
            power = power + moved * moved
    numer = jnp.zeros((inner_i, inner_x, TIME_SAMPLES), jnp.float32)
    denom = jnp.zeros((inner_i, inner_x, TIME_SAMPLES), jnp.float32)
    for window_step in range(2 * RT + 1):
        piece = stack[:, :, window_step:window_step + TIME_SAMPLES]
        numer = numer + piece * piece
        denom = denom + power[:, :, window_step:window_step + TIME_SAMPLES]
    semb = numer / (9.0 * denom + EPS)
    attr = semb * stack[:, :, RT:RT + TIME_SAMPLES] / 9.0
    return (semb, attr)

def attribute(volume, dip_il, dip_xl):
    padding = 2 * MAX_DIP_STEP + RT
    padded = jnp.pad(volume, ((1, 1), (1, 1), (padding, padding)))
    return attribute_padded(padded, dip_il, dip_xl)

def correlate(monitor, baseline):
    half_lags = LAGS // 2
    inner_i, inner_x = (monitor.shape[0], monitor.shape[1])
    base_pad = jnp.pad(baseline, ((0, 0), (0, 0), (half_lags, half_lags)))
    mon_energy = lax.optimization_barrier(jnp.sum(monitor * monitor, axis=-1))
    base_energy = lax.optimization_barrier(jnp.sum(baseline * baseline, axis=-1))
    factor = NWIN / jnp.sqrt(mon_energy * base_energy + EPS)
    columns = []
    for lag_index in range(LAGS):
        product = monitor * base_pad[:, :, lag_index:lag_index + TIME_SAMPLES]
        columns.append(lax.optimization_barrier(jnp.sum(product.reshape(inner_i, inner_x, NWIN, TIME_SAMPLES // NWIN), axis=-1)))
    result = jnp.stack(columns, axis=2) * factor[:, :, None, None]
    return result.reshape(inner_i, inner_x, LAGS * NWIN)

def reference(amplitude, inline_slope, crossline_slope):
    _, base_attr = attribute(amplitude[0], inline_slope[0], crossline_slope[0])

    def one_vintage(items):
        semb, attr = attribute(items[0], items[1], items[2])
        return (semb, correlate(attr, base_attr))
    semb_all, correl_all = lax.map(one_vintage, (amplitude, inline_slope, crossline_slope))
    return (semb_all, correl_all)
```

```python
import jax
import jax.numpy as jnp
from jax import lax
from jax.experimental import pallas as pl
from jax.experimental.pallas import tpu as pltpu
from jax.sharding import PartitionSpec as P

TIME_SAMPLES = 256
MAX_DIP_STEP = 2
RT = 4
LAGS = 33
NWIN = 8
EPS = 1e-06

ROWS = 8
COLS = 16
TRACES = ROWS * COLS
PAD = 16
STEPS = (-1, 0, 1)


def steered(ref, lead, row, count, sign, dip):
    out = ref[lead, pl.ds(row, count), :]
    for k in range(-MAX_DIP_STEP, MAX_DIP_STEP + 1):
        if k:
            out = jnp.where(dip == k, ref[lead, pl.ds(row + sign * k, count), :], out)
    return out


def attr_kernel(tile, up, down, left, right, dip_il, dip_xl, semb_out, attr_out,
                rim, moved, inner, sums, three):
    rim[1:ROWS + 1, 1:COLS + 1, :] = tile[...]
    rim[0, 1:COLS + 1, :] = up[0]
    rim[ROWS + 1, 1:COLS + 1, :] = down[0]
    rim[:, 0:1, :] = left[...]
    rim[:, COLS + 1:COLS + 2, :] = right[...]
    zeros = jnp.zeros((PAD, TRACES), jnp.float32)
    for a in STEPS:
        for b in STEPS:
            n = 3 * (a + 1) + b + 1
            block = rim[1 + a:1 + a + ROWS, 1 + b:1 + b + COLS, :].reshape(TRACES, TIME_SAMPLES)
            moved[n, 0:PAD, :] = zeros
            moved[n, PAD + TIME_SAMPLES:, :] = zeros
            moved[n, PAD:PAD + TIME_SAMPLES, :] = block.T
    q = jnp.broadcast_to(dip_xl[...], (8, TRACES))
    p = jnp.broadcast_to(dip_il[...], (8, TRACES))
    for r in range(0, TIME_SAMPLES + 16, 8):
        for a in STEPS:
            n = 3 * (a + 1) + 1
            mid = moved[n, pl.ds(r + 8, 8), :]
            lo = steered(moved, n - 1, r + 8, 8, -1, q)
            hi = steered(moved, n + 1, r + 8, 8, 1, q)
            inner[2 * (a + 1), pl.ds(r, 8), :] = lo + mid + hi
            inner[2 * (a + 1) + 1, pl.ds(r, 8), :] = lo * lo + mid * mid + hi * hi
    for r in range(0, TIME_SAMPLES + 8, 8):
        total = []
        for part in (0, 1):
            total.append(
                inner[2 + part, pl.ds(r + 4, 8), :]
                + steered(inner, part, r + 4, 8, -1, p)
                + steered(inner, 4 + part, r + 4, 8, 1, p)
            )
        sums[0, pl.ds(r, 8), :] = total[0]
        sums[1, pl.ds(r, 8), :] = total[0] * total[0]
        sums[2, pl.ds(r, 8), :] = total[1]
    for r in range(0, TIME_SAMPLES, 8):
        numer = sums[1, pl.ds(r, 8), :]
        denom = sums[2, pl.ds(r, 8), :]
        for s in range(1, 2 * RT + 1):
            numer = numer + sums[1, pl.ds(r + s, 8), :]
            denom = denom + sums[2, pl.ds(r + s, 8), :]
        semb = numer / (9.0 * denom + EPS)
        three[pl.ds(r, 8), :] = semb
        attr_out[pl.ds(r, 8), :] = semb * sums[0, pl.ds(r + RT, 8), :] * (1.0 / 9.0)
    semb_out[...] = three[...].T.reshape(ROWS, COLS, TIME_SAMPLES)


def pair_sum(x, y, half, low):
    return jnp.where(low, x, pltpu.roll(y, half, 0)) + jnp.where(low, pltpu.roll(x, 8 - half, 0), y)


def correl_kernel(mon, own, far1, far2, far3, out, base, result):
    half_lags = LAGS // 2
    leader = lax.rem(lax.axis_index("vintage"), 4) == 0
    zeros = jnp.zeros((half_lags, TRACES), jnp.float32)
    base[0:half_lags, :] = zeros
    base[half_lags + TIME_SAMPLES:, :] = zeros

    @pl.when(leader)
    def _():
        base[half_lags:half_lags + TIME_SAMPLES, :] = own[...]

    @pl.when(jnp.logical_not(leader))
    def _():
        base[half_lags:half_lags + TIME_SAMPLES, :] = far1[...] + far2[...] + far3[...]

    mon_energy = jnp.zeros((8, TRACES), jnp.float32)
    base_energy = jnp.zeros((8, TRACES), jnp.float32)
    for r in range(0, TIME_SAMPLES, 8):
        m = mon[pl.ds(r, 8), :]
        b = base[pl.ds(half_lags + r, 8), :]
        mon_energy = mon_energy + m * m
        base_energy = base_energy + b * b
    mon_energy = jnp.sum(mon_energy, axis=0, keepdims=True)
    base_energy = jnp.sum(base_energy, axis=0, keepdims=True)
    factor = NWIN / jnp.sqrt(mon_energy * base_energy + EPS)
    sub = lax.broadcasted_iota(jnp.int32, (8, TRACES), 0)
    width = TIME_SAMPLES // NWIN
    for lag in range(LAGS):
        level = []
        for w in range(NWIN):
            acc = None
            for r in range(w * width, (w + 1) * width, 8):
                term = mon[pl.ds(r, 8), :] * base[pl.ds(r + lag, 8), :]
                acc = term if acc is None else acc + term
            level.append(acc)
        level = [pair_sum(level[w], level[w + 4], 4, sub < 4) for w in range(4)]
        level = [pair_sum(level[w], level[w + 2], 2, (sub & 2) == 0) for w in range(2)]
        row = pair_sum(level[0], level[1], 1, (sub & 1) == 0)
        result[pl.ds(lag * 8, 8), :] = row * factor
    out[...] = result[...].T.reshape(ROWS, COLS, LAGS * NWIN)


def vmem(n):
    return [pl.BlockSpec(memory_space=pltpu.VMEM)] * n


def attributes(tile, up, down, left, right, dip_il, dip_xl):
    return pl.pallas_call(
        attr_kernel,
        out_shape=(
            jax.ShapeDtypeStruct((ROWS, COLS, TIME_SAMPLES), jnp.float32),
            jax.ShapeDtypeStruct((TIME_SAMPLES, TRACES), jnp.float32),
        ),
        in_specs=vmem(7),
        out_specs=tuple(vmem(2)),
        scratch_shapes=[
            pltpu.VMEM((ROWS + 2, COLS + 8, TIME_SAMPLES), jnp.float32),
            pltpu.VMEM((9, TIME_SAMPLES + 2 * PAD, TRACES), jnp.float32),
            pltpu.VMEM((6, TIME_SAMPLES + 16, TRACES), jnp.float32),
            pltpu.VMEM((3, TIME_SAMPLES + 8, TRACES), jnp.float32),
            pltpu.VMEM((TIME_SAMPLES, TRACES), jnp.float32),
        ],
        compiler_params=pltpu.CompilerParams(vmem_limit_bytes=16 << 20),
        name="attributes",
    )(tile, up, down, left, right, dip_il, dip_xl)


def correlate(mon, own, far):
    return pl.pallas_call(
        correl_kernel,
        out_shape=jax.ShapeDtypeStruct((ROWS, COLS, LAGS * NWIN), jnp.float32),
        in_specs=vmem(5),
        out_specs=pl.BlockSpec(memory_space=pltpu.VMEM),
        scratch_shapes=[
            pltpu.VMEM((TIME_SAMPLES + LAGS - 1, TRACES), jnp.float32),
            pltpu.VMEM((LAGS * NWIN, TRACES), jnp.float32),
        ],
        compiler_params=pltpu.CompilerParams(vmem_limit_bytes=16 << 20),
        name="correlate",
    )(mon, own, *far)


def neighbours(block, axis, dim):
    count = lax.axis_size(axis)
    forward = [(i, i + 1) for i in range(count - 1)]
    backward = [(target, source) for source, target in forward]
    low = lax.ppermute(lax.slice_in_dim(block, block.shape[dim] - 1, None, axis=dim), axis, forward)
    high = lax.ppermute(lax.slice_in_dim(block, 0, 1, axis=dim), axis, backward)
    return low, high


def per_device(amplitude, inline_slope, crossline_slope):
    tile = amplitude[0]
    dip_il = inline_slope.reshape(1, TRACES)
    dip_xl = crossline_slope.reshape(1, TRACES)
    up, down = neighbours(tile, "inline", 0)
    left, right = neighbours(jnp.concatenate([up, tile, down], axis=0), "xline", 1)
    semb, attr = attributes(tile, up, down, left, right, dip_il, dip_xl)
    got = [lax.ppermute(attr, "vintage", [(0, k)]) for k in (8, 4, 12)]
    first = lax.axis_index("vintage") == 0
    own = jnp.where(first, attr, got[0] + got[1] + got[2])
    far = [lax.ppermute(own, "vintage", [(s, s + k) for s in (0, 4, 8, 12)]) for k in (3, 2, 1)]
    correl = correlate(attr, own, far)
    return (semb[None], correl[None])


def solution(mesh):
    return jax.shard_map(
        per_device,
        mesh=mesh,
        in_specs=(
            P("vintage", "inline", "xline", None),
            P("vintage", "inline", "xline"),
            P("vintage", "inline", "xline"),
        ),
        out_specs=(P("vintage", "inline", "xline", None), P("vintage", "inline", "xline", None)),
        check_vma=False,
    )
```

```python
import jax
import jax.numpy as jnp
from jax import lax
from jax.experimental import pallas as pl
from jax.experimental.pallas import tpu as pltpu
from jax.sharding import PartitionSpec as P

TIME_SAMPLES = 256
MAX_DIP_STEP = 2
RT = 4
LAGS = 33
NWIN = 8
EPS = 1e-06

ROWS = 8
COLS = 16
TRACES = ROWS * COLS
PAD = 16
STEPS = (-1, 0, 1)


def steered(ref, lead, row, count, sign, dip):
    out = ref[lead, pl.ds(row, count), :]
    for k in range(-MAX_DIP_STEP, MAX_DIP_STEP + 1):
        if k:
            out = jnp.where(dip == k, ref[lead, pl.ds(row + sign * k, count), :], out)
    return out


def first_kernel(*refs):
    @pl.when(lax.axis_index("vintage") == 0)
    def _():
        attr_body(*refs)


def later_kernel(*refs):
    ins, semb_first, attr_first, semb_out, attr_out = refs[:7], refs[7], refs[8], refs[9], refs[10]
    first = lax.axis_index("vintage") == 0

    @pl.when(first)
    def _():
        semb_out[...] = semb_first[...]
        attr_out[...] = attr_first[...]

    @pl.when(jnp.logical_not(first))
    def _():
        attr_body(*ins, *refs[9:])


def attr_body(tile, up, down, left, right, dip_il, dip_xl, semb_out, attr_out,
              rim, moved, inner, sums, three):
    rim[1:ROWS + 1, 1:COLS + 1, :] = tile[...]
    rim[0, 1:COLS + 1, :] = up[0]
    rim[ROWS + 1, 1:COLS + 1, :] = down[0]
    rim[:, 0:1, :] = left[...]
    rim[:, COLS + 1:COLS + 2, :] = right[...]
    zeros = jnp.zeros((PAD, TRACES), jnp.float32)
    for a in STEPS:
        for b in STEPS:
            n = 3 * (a + 1) + b + 1
            block = rim[1 + a:1 + a + ROWS, 1 + b:1 + b + COLS, :].reshape(TRACES, TIME_SAMPLES)
            moved[n, 0:PAD, :] = zeros
            moved[n, PAD + TIME_SAMPLES:, :] = zeros
            moved[n, PAD:PAD + TIME_SAMPLES, :] = block.T
    q = jnp.broadcast_to(dip_xl[...], (8, TRACES))
    p = jnp.broadcast_to(dip_il[...], (8, TRACES))
    for r in range(0, TIME_SAMPLES + 16, 8):
        for a in STEPS:
            n = 3 * (a + 1) + 1
            mid = moved[n, pl.ds(r + 8, 8), :]
            lo = steered(moved, n - 1, r + 8, 8, -1, q)
            hi = steered(moved, n + 1, r + 8, 8, 1, q)
            inner[2 * (a + 1), pl.ds(r, 8), :] = lo + mid + hi
            inner[2 * (a + 1) + 1, pl.ds(r, 8), :] = lo * lo + mid * mid + hi * hi
    for r in range(0, TIME_SAMPLES + 8, 8):
        total = []
        for part in (0, 1):
            total.append(
                inner[2 + part, pl.ds(r + 4, 8), :]
                + steered(inner, part, r + 4, 8, -1, p)
                + steered(inner, 4 + part, r + 4, 8, 1, p)
            )
        sums[0, pl.ds(r, 8), :] = total[0]
        sums[1, pl.ds(r, 8), :] = total[0] * total[0]
        sums[2, pl.ds(r, 8), :] = total[1]
    for r in range(0, TIME_SAMPLES, 8):
        numer = sums[1, pl.ds(r, 8), :]
        denom = sums[2, pl.ds(r, 8), :]
        for s in range(1, 2 * RT + 1):
            numer = numer + sums[1, pl.ds(r + s, 8), :]
            denom = denom + sums[2, pl.ds(r + s, 8), :]
        semb = numer / (9.0 * denom + EPS)
        three[pl.ds(r, 8), :] = semb
        attr_out[pl.ds(r, 8), :] = semb * sums[0, pl.ds(r + RT, 8), :] * (1.0 / 9.0)
    semb_out[...] = three[...].T.reshape(ROWS, COLS, TIME_SAMPLES)


def pair_sum(x, y, half, low):
    return jnp.where(low, x, pltpu.roll(y, half, 0)) + jnp.where(low, pltpu.roll(x, 8 - half, 0), y)


def correl_kernel(mon, held, near, out, base, result):
    half_lags = LAGS // 2
    odd = lax.rem(lax.axis_index("vintage"), 2) == 1
    zeros = jnp.zeros((half_lags, TRACES), jnp.float32)
    base[0:half_lags, :] = zeros
    base[half_lags + TIME_SAMPLES:, :] = zeros

    @pl.when(odd)
    def _():
        base[half_lags:half_lags + TIME_SAMPLES, :] = near[...]

    @pl.when(jnp.logical_not(odd))
    def _():
        base[half_lags:half_lags + TIME_SAMPLES, :] = held[...]

    mon_energy = jnp.zeros((8, TRACES), jnp.float32)
    base_energy = jnp.zeros((8, TRACES), jnp.float32)
    for r in range(0, TIME_SAMPLES, 8):
        m = mon[pl.ds(r, 8), :]
        b = base[pl.ds(half_lags + r, 8), :]
        mon_energy = mon_energy + m * m
        base_energy = base_energy + b * b
    mon_energy = jnp.sum(mon_energy, axis=0, keepdims=True)
    base_energy = jnp.sum(base_energy, axis=0, keepdims=True)
    factor = NWIN / jnp.sqrt(mon_energy * base_energy + EPS)
    sub = lax.broadcasted_iota(jnp.int32, (8, TRACES), 0)
    width = TIME_SAMPLES // NWIN
    for lag in range(LAGS):
        level = []
        for w in range(NWIN):
            acc = None
            for r in range(w * width, (w + 1) * width, 8):
                term = mon[pl.ds(r, 8), :] * base[pl.ds(r + lag, 8), :]
                acc = term if acc is None else acc + term
            level.append(acc)
        level = [pair_sum(level[w], level[w + 4], 4, sub < 4) for w in range(4)]
        level = [pair_sum(level[w], level[w + 2], 2, (sub & 2) == 0) for w in range(2)]
        row = pair_sum(level[0], level[1], 1, (sub & 1) == 0)
        result[pl.ds(lag * 8, 8), :] = row * factor
    out[...] = result[...].T.reshape(ROWS, COLS, LAGS * NWIN)


def vmem(n):
    return [pl.BlockSpec(memory_space=pltpu.VMEM)] * n


def attributes(kernel, name, *args):
    return pl.pallas_call(
        kernel,
        out_shape=(
            jax.ShapeDtypeStruct((ROWS, COLS, TIME_SAMPLES), jnp.float32),
            jax.ShapeDtypeStruct((TIME_SAMPLES, TRACES), jnp.float32),
        ),
        in_specs=vmem(len(args)),
        out_specs=tuple(vmem(2)),
        scratch_shapes=[
            pltpu.VMEM((ROWS + 2, COLS + 8, TIME_SAMPLES), jnp.float32),
            pltpu.VMEM((9, TIME_SAMPLES + 2 * PAD, TRACES), jnp.float32),
            pltpu.VMEM((6, TIME_SAMPLES + 16, TRACES), jnp.float32),
            pltpu.VMEM((3, TIME_SAMPLES + 8, TRACES), jnp.float32),
            pltpu.VMEM((TIME_SAMPLES, TRACES), jnp.float32),
        ],
        compiler_params=pltpu.CompilerParams(vmem_limit_bytes=16 << 20),
        name=name,
    )(*args)


def correlate(mon, held, near):
    return pl.pallas_call(
        correl_kernel,
        out_shape=jax.ShapeDtypeStruct((ROWS, COLS, LAGS * NWIN), jnp.float32),
        in_specs=vmem(3),
        out_specs=pl.BlockSpec(memory_space=pltpu.VMEM),
        scratch_shapes=[
            pltpu.VMEM((TIME_SAMPLES + LAGS - 1, TRACES), jnp.float32),
            pltpu.VMEM((LAGS * NWIN, TRACES), jnp.float32),
        ],
        compiler_params=pltpu.CompilerParams(vmem_limit_bytes=16 << 20),
        name="correlate",
    )(mon, held, near)


def exchange(last, first, axis, planes):
    count = lax.axis_size(axis)
    steps = [(v * count + i, v * count + i + 1) for v in planes for i in range(count - 1)]
    low = lax.ppermute(last, ("vintage", axis), steps)
    high = lax.ppermute(first, ("vintage", axis), [(target, source) for source, target in steps])
    return low, high


def rim_of(tile, last, first, planes):
    up, down = exchange(last, first, "inline", planes)
    wide = jnp.concatenate([up, tile, down], axis=0)
    left, right = exchange(wide[:, -1:], wide[:, :1], "xline", planes)
    return up, down, left, right


def per_device(amplitude, inline_slope, crossline_slope):
    tile = amplitude[0]
    dips = (inline_slope.reshape(1, TRACES), crossline_slope.reshape(1, TRACES))
    vintages = lax.axis_size("vintage")
    place = lax.axis_index("vintage")
    last, first = tile[-1:], tile[:1]
    semb0, attr0 = attributes(first_kernel, "baseline", tile, *rim_of(tile, last, first, [0]), *dips)
    got = [lax.ppermute(attr0, "vintage", [(0, k)]) for k in (8, 4, 12)]
    last, first, attr0 = lax.optimization_barrier((last, first, attr0))
    rim = rim_of(tile, last, first, range(1, vintages))
    semb, attr = attributes(later_kernel, "monitor", tile, *rim, *dips, semb0, attr0)
    got = lax.optimization_barrier((*got, attr))[:3]
    held = jnp.where(place == 0, attr0, got[0] + got[1] + got[2])
    half = lax.ppermute(held, "vintage", [(s, s + 2) for s in range(0, vintages, 4)])
    held = jnp.where(lax.rem(place, 4) == 0, held, half)
    near = lax.ppermute(held, "vintage", [(s, s + 1) for s in range(0, vintages, 2)])
    correl = correlate(attr, held, near)
    return (semb[None], correl[None])


def solution(mesh):
    return jax.shard_map(
        per_device,
        mesh=mesh,
        in_specs=(
            P("vintage", "inline", "xline", None),
            P("vintage", "inline", "xline"),
            P("vintage", "inline", "xline"),
        ),
        out_specs=(P("vintage", "inline", "xline", None), P("vintage", "inline", "xline", None)),
        check_vma=False,
    )
```

```python
import jax
import jax.numpy as jnp
from jax import lax
from jax.experimental import pallas as pl
from jax.experimental.pallas import tpu as pltpu
from jax.sharding import PartitionSpec as P

TIME_SAMPLES = 256
MAX_DIP_STEP = 2
RT = 4
LAGS = 33
NWIN = 8
EPS = 1e-06
F = (0, 0, 0, 1)
TT = (12, 4, 8)


def FLIP(x, f):
    return tuple(x)[::-1] if f else tuple(x)


ROWS = 8
COLS = 16
TRACES = ROWS * COLS
PAD = 16
STEPS = (-1, 0, 1)


def steered(ref, lead, row, count, sign, dip):
    out = ref[lead, pl.ds(row, count), :]
    for k in range(-MAX_DIP_STEP, MAX_DIP_STEP + 1):
        if k:
            out = jnp.where(dip == k, ref[lead, pl.ds(row + sign * k, count), :], out)
    return out


def first_kernel(*refs):
    @pl.when(lax.axis_index("vintage") == 0)
    def _():
        r = refs
        attr_body(r[0], *FLIP(r[1:3], F[0]), *FLIP(r[3:5], F[1]), *r[5:])


def later_kernel(*refs):
    ins, semb_first, attr_first, semb_out, attr_out = refs[:7], refs[7], refs[8], refs[9], refs[10]
    first = lax.axis_index("vintage") == 0

    @pl.when(first)
    def _():
        semb_out[...] = semb_first[...]
        attr_out[...] = attr_first[...]

    @pl.when(jnp.logical_not(first))
    def _():
        r = ins
        attr_body(r[0], *FLIP(r[1:3], F[2]), *FLIP(r[3:5], F[3]), *r[5:], *refs[9:])


def attr_body(tile, row_a, row_b, col_a, col_b, dip_il, dip_xl, semb_out, attr_out,
              rim, moved, inner, sums, three):
    odd_row = lax.rem(lax.axis_index("inline"), 2) == 1
    odd_col = lax.rem(lax.axis_index("xline"), 2) == 1
    rim[1:ROWS + 1, 1:COLS + 1, :] = tile[...]
    rim[0, 1:COLS + 1, :] = jnp.where(odd_row, row_a[0], row_b[0])
    rim[ROWS + 1, 1:COLS + 1, :] = jnp.where(odd_row, row_b[0], row_a[0])
    rim[:, 0:1, :] = jnp.where(odd_col, col_a[...], col_b[...])
    rim[:, COLS + 1:COLS + 2, :] = jnp.where(odd_col, col_b[...], col_a[...])
    zeros = jnp.zeros((PAD, TRACES), jnp.float32)
    for a in STEPS:
        for b in STEPS:
            n = 3 * (a + 1) + b + 1
            block = rim[1 + a:1 + a + ROWS, 1 + b:1 + b + COLS, :].reshape(TRACES, TIME_SAMPLES)
            moved[n, 0:PAD, :] = zeros
            moved[n, PAD + TIME_SAMPLES:, :] = zeros
            moved[n, PAD:PAD + TIME_SAMPLES, :] = block.T
    q = jnp.broadcast_to(dip_xl[...], (8, TRACES))
    p = jnp.broadcast_to(dip_il[...], (8, TRACES))
    for r in range(0, TIME_SAMPLES + 16, 8):
        for a in STEPS:
            n = 3 * (a + 1) + 1
            mid = moved[n, pl.ds(r + 8, 8), :]
            lo = steered(moved, n - 1, r + 8, 8, -1, q)
            hi = steered(moved, n + 1, r + 8, 8, 1, q)
            inner[2 * (a + 1), pl.ds(r, 8), :] = lo + mid + hi
            inner[2 * (a + 1) + 1, pl.ds(r, 8), :] = lo * lo + mid * mid + hi * hi
    for r in range(0, TIME_SAMPLES + 8, 8):
        total = []
        for part in (0, 1):
            total.append(
                inner[2 + part, pl.ds(r + 4, 8), :]
                + steered(inner, part, r + 4, 8, -1, p)
                + steered(inner, 4 + part, r + 4, 8, 1, p)
            )
        sums[0, pl.ds(r, 8), :] = total[0]
        sums[1, pl.ds(r, 8), :] = total[0] * total[0]
        sums[2, pl.ds(r, 8), :] = total[1]
    for r in range(0, TIME_SAMPLES, 8):
        numer = sums[1, pl.ds(r, 8), :]
        denom = sums[2, pl.ds(r, 8), :]
        for s in range(1, 2 * RT + 1):
            numer = numer + sums[1, pl.ds(r + s, 8), :]
            denom = denom + sums[2, pl.ds(r + s, 8), :]
        semb = numer / (9.0 * denom + EPS)
        three[pl.ds(r, 8), :] = semb
        attr_out[pl.ds(r, 8), :] = semb * sums[0, pl.ds(r + RT, 8), :] * (1.0 / 9.0)
    semb_out[...] = three[...].T.reshape(ROWS, COLS, TIME_SAMPLES)


def pair_sum(x, y, half, low):
    return jnp.where(low, x, pltpu.roll(y, half, 0)) + jnp.where(low, pltpu.roll(x, 8 - half, 0), y)


def correl_kernel(mon, held, far3, far2, far1, out, base, result):
    half_lags = LAGS // 2
    holder = lax.rem(lax.axis_index("vintage"), 4) == 0
    zeros = jnp.zeros((half_lags, TRACES), jnp.float32)
    base[0:half_lags, :] = zeros
    base[half_lags + TIME_SAMPLES:, :] = zeros

    @pl.when(holder)
    def _():
        base[half_lags:half_lags + TIME_SAMPLES, :] = held[...]

    @pl.when(jnp.logical_not(holder))
    def _():
        base[half_lags:half_lags + TIME_SAMPLES, :] = far1[...] + far2[...] + far3[...]

    mon_energy = jnp.zeros((8, TRACES), jnp.float32)
    base_energy = jnp.zeros((8, TRACES), jnp.float32)
    for r in range(0, TIME_SAMPLES, 8):
        m = mon[pl.ds(r, 8), :]
        b = base[pl.ds(half_lags + r, 8), :]
        mon_energy = mon_energy + m * m
        base_energy = base_energy + b * b
    mon_energy = jnp.sum(mon_energy, axis=0, keepdims=True)
    base_energy = jnp.sum(base_energy, axis=0, keepdims=True)
    factor = NWIN / jnp.sqrt(mon_energy * base_energy + EPS)
    sub = lax.broadcasted_iota(jnp.int32, (8, TRACES), 0)
    width = TIME_SAMPLES // NWIN
    for lag in range(LAGS):
        level = []
        for w in range(NWIN):
            acc = None
            for r in range(w * width, (w + 1) * width, 8):
                term = mon[pl.ds(r, 8), :] * base[pl.ds(r + lag, 8), :]
                acc = term if acc is None else acc + term
            level.append(acc)
        level = [pair_sum(level[w], level[w + 4], 4, sub < 4) for w in range(4)]
        level = [pair_sum(level[w], level[w + 2], 2, (sub & 2) == 0) for w in range(2)]
        row = pair_sum(level[0], level[1], 1, (sub & 1) == 0)
        result[pl.ds(lag * 8, 8), :] = row * factor
    out[...] = result[...].T.reshape(ROWS, COLS, LAGS * NWIN)


def vmem(n):
    return [pl.BlockSpec(memory_space=pltpu.VMEM)] * n


def attributes(kernel, name, *args):
    return pl.pallas_call(
        kernel,
        out_shape=(
            jax.ShapeDtypeStruct((ROWS, COLS, TIME_SAMPLES), jnp.float32),
            jax.ShapeDtypeStruct((TIME_SAMPLES, TRACES), jnp.float32),
        ),
        in_specs=vmem(len(args)),
        out_specs=tuple(vmem(2)),
        scratch_shapes=[
            pltpu.VMEM((ROWS + 2, COLS + 8, TIME_SAMPLES), jnp.float32),
            pltpu.VMEM((9, TIME_SAMPLES + 2 * PAD, TRACES), jnp.float32),
            pltpu.VMEM((6, TIME_SAMPLES + 16, TRACES), jnp.float32),
            pltpu.VMEM((3, TIME_SAMPLES + 8, TRACES), jnp.float32),
            pltpu.VMEM((TIME_SAMPLES, TRACES), jnp.float32),
        ],
        compiler_params=pltpu.CompilerParams(vmem_limit_bytes=16 << 20),
        name=name,
    )(*args)


def correlate(mon, held, far):
    return pl.pallas_call(
        correl_kernel,
        out_shape=jax.ShapeDtypeStruct((ROWS, COLS, LAGS * NWIN), jnp.float32),
        in_specs=vmem(5),
        out_specs=pl.BlockSpec(memory_space=pltpu.VMEM),
        scratch_shapes=[
            pltpu.VMEM((TIME_SAMPLES + LAGS - 1, TRACES), jnp.float32),
            pltpu.VMEM((LAGS * NWIN, TRACES), jnp.float32),
        ],
        compiler_params=pltpu.CompilerParams(vmem_limit_bytes=16 << 20),
        name="correlate",
    )(mon, held, *far)


def pair_sends(first, last, axis):
    odd = lax.rem(lax.axis_index(axis), 2) == 1
    return jnp.where(odd, first, last), jnp.where(odd, last, first)


def swap(sends, axis, planes):
    count = lax.axis_size(axis)
    out = []
    for start, send in enumerate(sends):
        low = [(v * count + i, v * count + i + 1) for v in planes for i in range(start, count - 1, 2)]
        out.append(lax.ppermute(send, ("vintage", axis), low + [(b, a) for a, b in low]))
    return out


def edge_columns(tile, rows):
    odd = lax.rem(lax.axis_index("inline"), 2) == 1
    above, below = jnp.where(odd, rows[0], rows[1]), jnp.where(odd, rows[1], rows[0])
    first, last = (
        jnp.concatenate([above[:, j:j + 1], tile[:, j:j + 1], below[:, j:j + 1]], axis=0)
        for j in (0, COLS - 1)
    )
    return pair_sends(first, last, "xline")


def per_device(amplitude, inline_slope, crossline_slope):
    tile = amplitude[0]
    dips = (inline_slope.reshape(1, TRACES), crossline_slope.reshape(1, TRACES))
    vintages = lax.axis_size("vintage")
    others = range(1, vintages)
    sends = pair_sends(tile[:1], tile[-1:], "inline")
    rows = swap(sends, "inline", [0])
    cols = edge_columns(tile, rows)
    gated = lax.optimization_barrier((*cols, *sends))
    cols, sends = gated[:2], gated[2:]
    cols = swap(cols, "xline", [0])
    semb0, attr0 = attributes(first_kernel, "baseline", tile, *FLIP(rows, F[0]), *FLIP(cols, F[1]), *dips)
    got = [lax.ppermute(attr0, "vintage", [(0, k)]) for k in TT]
    rows = swap(sends, "inline", others)
    cols = swap(edge_columns(tile, rows), "xline", others)
    semb, attr = attributes(later_kernel, "monitor", tile, *FLIP(rows, F[2]), *FLIP(cols, F[3]), *dips, semb0, attr0)
    got = lax.optimization_barrier((*got, attr))[:3]
    held = jnp.where(lax.axis_index("vintage") == 0, attr0, got[0] + got[1] + got[2])
    far = [lax.ppermute(held, "vintage", [(s, s + k) for s in range(0, vintages, 4)]) for k in (1, 2, 3)]
    correl = correlate(attr, held, far)
    return (semb[None], correl[None])


def solution(mesh):
    return jax.shard_map(
        per_device,
        mesh=mesh,
        in_specs=(
            P("vintage", "inline", "xline", None),
            P("vintage", "inline", "xline"),
            P("vintage", "inline", "xline"),
        ),
        out_specs=(P("vintage", "inline", "xline", None), P("vintage", "inline", "xline", None)),
        check_vma=False,
    )
```

```python
import functools

import jax
import jax.numpy as jnp
from jax import lax
from jax.experimental import pallas as pl
from jax.experimental.pallas import tpu as pltpu
from jax.sharding import PartitionSpec as P

TIME_SAMPLES = 256
MAX_DIP_STEP = 2
RT = 4
LAGS = 33
NWIN = 8
EPS = 1e-06

HEAD = 0, 1, 2, 14
FANOUT = {0: (8, 4, 12), 1: (9, 5, 13), 2: (6, 7, 3), 14: (10, 11, 15)}
ROWS = 8
COLS = 16
TRACES = ROWS * COLS
PAD = 16
STEPS = (-1, 0, 1)


def steered(ref, lead, row, count, sign, dip):
    out = ref[lead, pl.ds(row, count), :]
    for k in range(-MAX_DIP_STEP, MAX_DIP_STEP + 1):
        if k:
            out = jnp.where(dip == k, ref[lead, pl.ds(row + sign * k, count), :], out)
    return out


def is_head(place):
    return functools.reduce(jnp.logical_or, [place == v for v in HEAD])


def first_kernel(*refs):
    @pl.when(is_head(lax.axis_index("vintage")))
    def _():
        attr_body(refs[0], refs[1], refs[2], refs[4], refs[3], *refs[5:])


def later_kernel(*refs):
    ins, semb_first, attr_first, semb_out, attr_out = refs[:7], refs[7], refs[8], refs[9], refs[10]
    head = is_head(lax.axis_index("vintage"))

    @pl.when(head)
    def _():
        semb_out[...] = semb_first[...]
        attr_out[...] = attr_first[...]

    @pl.when(jnp.logical_not(head))
    def _():
        attr_body(*ins, *refs[9:])


def attr_body(tile, row_a, row_b, col_a, col_b, dip_il, dip_xl, semb_out, attr_out,
              rim, moved, inner, sums, three):
    odd_row = lax.rem(lax.axis_index("inline"), 2) == 1
    odd_col = lax.rem(lax.axis_index("xline"), 2) == 1
    rim[1:ROWS + 1, 1:COLS + 1, :] = tile[...]
    rim[0, 1:COLS + 1, :] = jnp.where(odd_row, row_a[0], row_b[0])
    rim[ROWS + 1, 1:COLS + 1, :] = jnp.where(odd_row, row_b[0], row_a[0])
    rim[:, 0:1, :] = jnp.where(odd_col, col_a[...], col_b[...])
    rim[:, COLS + 1:COLS + 2, :] = jnp.where(odd_col, col_b[...], col_a[...])
    zeros = jnp.zeros((PAD, TRACES), jnp.float32)
    for a in STEPS:
        for b in STEPS:
            n = 3 * (a + 1) + b + 1
            block = rim[1 + a:1 + a + ROWS, 1 + b:1 + b + COLS, :].reshape(TRACES, TIME_SAMPLES)
            moved[n, 0:PAD, :] = zeros
            moved[n, PAD + TIME_SAMPLES:, :] = zeros
            moved[n, PAD:PAD + TIME_SAMPLES, :] = block.T
    q = jnp.broadcast_to(dip_xl[...], (8, TRACES))
    p = jnp.broadcast_to(dip_il[...], (8, TRACES))
    for r in range(0, TIME_SAMPLES + 16, 8):
        for a in STEPS:
            n = 3 * (a + 1) + 1
            mid = moved[n, pl.ds(r + 8, 8), :]
            lo = steered(moved, n - 1, r + 8, 8, -1, q)
            hi = steered(moved, n + 1, r + 8, 8, 1, q)
            inner[2 * (a + 1), pl.ds(r, 8), :] = lo + mid + hi
            inner[2 * (a + 1) + 1, pl.ds(r, 8), :] = lo * lo + mid * mid + hi * hi
    for r in range(0, TIME_SAMPLES + 8, 8):
        total = []
        for part in (0, 1):
            total.append(
                inner[2 + part, pl.ds(r + 4, 8), :]
                + steered(inner, part, r + 4, 8, -1, p)
                + steered(inner, 4 + part, r + 4, 8, 1, p)
            )
        sums[0, pl.ds(r, 8), :] = total[0]
        sums[1, pl.ds(r, 8), :] = total[0] * total[0]
        sums[2, pl.ds(r, 8), :] = total[1]
    for r in range(0, TIME_SAMPLES, 8):
        numer = sums[1, pl.ds(r, 8), :]
        denom = sums[2, pl.ds(r, 8), :]
        for s in range(1, 2 * RT + 1):
            numer = numer + sums[1, pl.ds(r + s, 8), :]
            denom = denom + sums[2, pl.ds(r + s, 8), :]
        semb = numer / (9.0 * denom + EPS)
        three[pl.ds(r, 8), :] = semb
        attr_out[pl.ds(r, 8), :] = semb * sums[0, pl.ds(r + RT, 8), :] * (1.0 / 9.0)
    semb_out[...] = three[...].T.reshape(ROWS, COLS, TIME_SAMPLES)


def pair_sum(x, y, half, low):
    return jnp.where(low, x, pltpu.roll(y, half, 0)) + jnp.where(low, pltpu.roll(x, 8 - half, 0), y)


def correl_kernel(mon, held, far3, far2, far1, out, base, result):
    half_lags = LAGS // 2
    holder = is_head(lax.axis_index("vintage"))
    zeros = jnp.zeros((half_lags, TRACES), jnp.float32)
    base[0:half_lags, :] = zeros
    base[half_lags + TIME_SAMPLES:, :] = zeros

    @pl.when(holder)
    def _():
        base[half_lags:half_lags + TIME_SAMPLES, :] = held[...]

    @pl.when(jnp.logical_not(holder))
    def _():
        base[half_lags:half_lags + TIME_SAMPLES, :] = far1[...] + far2[...] + far3[...]

    mon_energy = jnp.zeros((8, TRACES), jnp.float32)
    base_energy = jnp.zeros((8, TRACES), jnp.float32)
    for r in range(0, TIME_SAMPLES, 8):
        m = mon[pl.ds(r, 8), :]
        b = base[pl.ds(half_lags + r, 8), :]
        mon_energy = mon_energy + m * m
        base_energy = base_energy + b * b
    mon_energy = jnp.sum(mon_energy, axis=0, keepdims=True)
    base_energy = jnp.sum(base_energy, axis=0, keepdims=True)
    factor = NWIN / jnp.sqrt(mon_energy * base_energy + EPS)
    sub = lax.broadcasted_iota(jnp.int32, (8, TRACES), 0)
    width = TIME_SAMPLES // NWIN
    for lag in range(LAGS):
        level = []
        for w in range(NWIN):
            acc = None
            for r in range(w * width, (w + 1) * width, 8):
                term = mon[pl.ds(r, 8), :] * base[pl.ds(r + lag, 8), :]
                acc = term if acc is None else acc + term
            level.append(acc)
        level = [pair_sum(level[w], level[w + 4], 4, sub < 4) for w in range(4)]
        level = [pair_sum(level[w], level[w + 2], 2, (sub & 2) == 0) for w in range(2)]
        row = pair_sum(level[0], level[1], 1, (sub & 1) == 0)
        result[pl.ds(lag * 8, 8), :] = row * factor
    out[...] = result[...].T.reshape(ROWS, COLS, LAGS * NWIN)


def vmem(n):
    return [pl.BlockSpec(memory_space=pltpu.VMEM)] * n


def attributes(kernel, name, *args):
    return pl.pallas_call(
        kernel,
        out_shape=(
            jax.ShapeDtypeStruct((ROWS, COLS, TIME_SAMPLES), jnp.float32),
            jax.ShapeDtypeStruct((TIME_SAMPLES, TRACES), jnp.float32),
        ),
        in_specs=vmem(len(args)),
        out_specs=tuple(vmem(2)),
        scratch_shapes=[
            pltpu.VMEM((ROWS + 2, COLS + 8, TIME_SAMPLES), jnp.float32),
            pltpu.VMEM((9, TIME_SAMPLES + 2 * PAD, TRACES), jnp.float32),
            pltpu.VMEM((6, TIME_SAMPLES + 16, TRACES), jnp.float32),
            pltpu.VMEM((3, TIME_SAMPLES + 8, TRACES), jnp.float32),
            pltpu.VMEM((TIME_SAMPLES, TRACES), jnp.float32),
        ],
        compiler_params=pltpu.CompilerParams(vmem_limit_bytes=16 << 20),
        name=name,
    )(*args)


def correlate(mon, held, far):
    return pl.pallas_call(
        correl_kernel,
        out_shape=jax.ShapeDtypeStruct((ROWS, COLS, LAGS * NWIN), jnp.float32),
        in_specs=vmem(5),
        out_specs=pl.BlockSpec(memory_space=pltpu.VMEM),
        scratch_shapes=[
            pltpu.VMEM((TIME_SAMPLES + LAGS - 1, TRACES), jnp.float32),
            pltpu.VMEM((LAGS * NWIN, TRACES), jnp.float32),
        ],
        compiler_params=pltpu.CompilerParams(vmem_limit_bytes=16 << 20),
        name="correlate",
    )(mon, held, *far)


def pair_sends(first, last, axis):
    odd = lax.rem(lax.axis_index(axis), 2) == 1
    return jnp.where(odd, first, last), jnp.where(odd, last, first)


def swap(sends, axis, planes):
    count = lax.axis_size(axis)
    out = []
    for start, send in enumerate(sends):
        low = [(v * count + i, v * count + i + 1) for v in planes for i in range(start, count - 1, 2)]
        out.append(lax.ppermute(send, ("vintage", axis), low + [(b, a) for a, b in low]))
    return out


def edge_columns(ends, rows):
    odd = lax.rem(lax.axis_index("inline"), 2) == 1
    above, below = jnp.where(odd, rows[0], rows[1]), jnp.where(odd, rows[1], rows[0])
    first, last = (
        jnp.concatenate([above[:, j:j + 1], end, below[:, j:j + 1]], axis=0)
        for j, end in zip((0, COLS - 1), ends)
    )
    return pair_sends(first, last, "xline")


def per_device(amplitude, inline_slope, crossline_slope):
    tile = amplitude[0]
    dips = (inline_slope.reshape(1, TRACES), crossline_slope.reshape(1, TRACES))
    others = [v for v in range(lax.axis_size("vintage")) if v not in HEAD]
    sends = pair_sends(tile[:1], tile[-1:], "inline")
    rows = swap(sends, "inline", HEAD)
    gated = lax.optimization_barrier((*sends[::-1], tile[:, :1], tile[:, -1:]))
    ends, sends = gated[2:], gated[1::-1]
    cols = swap(edge_columns(ends, rows), "xline", HEAD)
    semb0, attr0 = attributes(first_kernel, "head", tile, *rows, *cols[::-1], *dips)
    got = [lax.ppermute(attr0, "vintage", [(0, k)]) for k in (1, 14, 2)]
    held = jnp.where(lax.axis_index("vintage") == 0, attr0, got[0] + got[1] + got[2])
    far = [
        lax.ppermute(held, "vintage", [(s, FANOUT[s][n]) for s in HEAD])
        for n in (2, 1, 0)
    ]
    rows = swap(sends, "inline", others)
    cols = edge_columns(ends, rows)
    cols = lax.optimization_barrier((*cols, held))[:2]
    cols = swap(cols, "xline", others)
    semb, attr = attributes(later_kernel, "tail", tile, *rows, *cols, *dips, semb0, attr0)
    correl = correlate(attr, held, far)
    return (semb[None], correl[None])


def solution(mesh):
    return jax.shard_map(
        per_device,
        mesh=mesh,
        in_specs=(
            P("vintage", "inline", "xline", None),
            P("vintage", "inline", "xline"),
            P("vintage", "inline", "xline"),
        ),
        out_specs=(P("vintage", "inline", "xline", None), P("vintage", "inline", "xline", None)),
        check_vma=False,
    )
```

```python
import jax
import jax.numpy as jnp
from jax import lax
from jax.experimental import pallas as pl
from jax.experimental.pallas import tpu as pltpu
from jax.sharding import PartitionSpec as P

TIME_SAMPLES = 256
MAX_DIP_STEP = 2
RT = 4
LAGS = 33
NWIN = 8
EPS = 1e-06

HOLDERS = 0, 4, 8, 12
ROWS = 8
COLS = 16
TRACES = ROWS * COLS
PAD = 16
STEPS = (-1, 0, 1)


def steered(ref, lead, row, count, sign, dip):
    out = ref[lead, pl.ds(row, count), :]
    for k in range(-MAX_DIP_STEP, MAX_DIP_STEP + 1):
        if k:
            out = jnp.where(dip == k, ref[lead, pl.ds(row + sign * k, count), :], out)
    return out


def first_kernel(*refs):
    @pl.when(lax.axis_index("vintage") == 0)
    def _():
        attr_body(*refs[:4], refs[5], refs[4], *refs[6:])


def later_kernel(*refs):
    ins, semb_first, attr_first, semb_out, attr_out = refs[:8], refs[8], refs[9], refs[10], refs[11]
    head = lax.axis_index("vintage") == 0

    @pl.when(head)
    def _():
        semb_out[...] = semb_first[...]
        attr_out[...] = attr_first[...]

    @pl.when(jnp.logical_not(head))
    def _():
        attr_body(*ins, *refs[10:])


def attr_body(tile, row_01, row_12, row_23, col_a, col_b, dip_il, dip_xl, semb_out, attr_out,
              rim, moved, inner, sums, three):
    odd_row = lax.rem(lax.axis_index("inline"), 2) == 1
    odd_col = lax.rem(lax.axis_index("xline"), 2) == 1
    rim[1:ROWS + 1, 1:COLS + 1, :] = tile[...]
    row_a, row_b = row_01[0] + row_23[0], row_12[0]
    rim[0, 1:COLS + 1, :] = jnp.where(odd_row, row_a, row_b)
    rim[ROWS + 1, 1:COLS + 1, :] = jnp.where(odd_row, row_b, row_a)
    rim[:, 0:1, :] = jnp.where(odd_col, col_a[...], col_b[...])
    rim[:, COLS + 1:COLS + 2, :] = jnp.where(odd_col, col_b[...], col_a[...])
    zeros = jnp.zeros((PAD, TRACES), jnp.float32)
    for a in STEPS:
        for b in STEPS:
            n = 3 * (a + 1) + b + 1
            block = rim[1 + a:1 + a + ROWS, 1 + b:1 + b + COLS, :].reshape(TRACES, TIME_SAMPLES)
            moved[n, 0:PAD, :] = zeros
            moved[n, PAD + TIME_SAMPLES:, :] = zeros
            moved[n, PAD:PAD + TIME_SAMPLES, :] = block.T
    q = jnp.broadcast_to(dip_xl[...], (8, TRACES))
    p = jnp.broadcast_to(dip_il[...], (8, TRACES))
    for r in range(0, TIME_SAMPLES + 16, 8):
        for a in STEPS:
            n = 3 * (a + 1) + 1
            mid = moved[n, pl.ds(r + 8, 8), :]
            lo = steered(moved, n - 1, r + 8, 8, -1, q)
            hi = steered(moved, n + 1, r + 8, 8, 1, q)
            inner[2 * (a + 1), pl.ds(r, 8), :] = lo + mid + hi
            inner[2 * (a + 1) + 1, pl.ds(r, 8), :] = lo * lo + mid * mid + hi * hi
    for r in range(0, TIME_SAMPLES + 8, 8):
        total = []
        for part in (0, 1):
            total.append(
                inner[2 + part, pl.ds(r + 4, 8), :]
                + steered(inner, part, r + 4, 8, -1, p)
                + steered(inner, 4 + part, r + 4, 8, 1, p)
            )
        sums[0, pl.ds(r, 8), :] = total[0]
        sums[1, pl.ds(r, 8), :] = total[0] * total[0]
        sums[2, pl.ds(r, 8), :] = total[1]
    for r in range(0, TIME_SAMPLES, 8):
        numer = sums[1, pl.ds(r, 8), :]
        denom = sums[2, pl.ds(r, 8), :]
        for s in range(1, 2 * RT + 1):
            numer = numer + sums[1, pl.ds(r + s, 8), :]
            denom = denom + sums[2, pl.ds(r + s, 8), :]
        semb = numer / (9.0 * denom + EPS)
        three[pl.ds(r, 8), :] = semb
        attr_out[pl.ds(r, 8), :] = semb * sums[0, pl.ds(r + RT, 8), :] * (1.0 / 9.0)
    semb_out[...] = three[...].T.reshape(ROWS, COLS, TIME_SAMPLES)


def pair_sum(x, y, half, low):
    return jnp.where(low, x, pltpu.roll(y, half, 0)) + jnp.where(low, pltpu.roll(x, 8 - half, 0), y)


def correl_kernel(mon, held, far3, far2, far1, out, base, result):
    half_lags = LAGS // 2
    holder = lax.rem(lax.axis_index("vintage"), 4) == 0
    zeros = jnp.zeros((half_lags, TRACES), jnp.float32)
    base[0:half_lags, :] = zeros
    base[half_lags + TIME_SAMPLES:, :] = zeros

    @pl.when(holder)
    def _():
        base[half_lags:half_lags + TIME_SAMPLES, :] = held[...]

    @pl.when(jnp.logical_not(holder))
    def _():
        base[half_lags:half_lags + TIME_SAMPLES, :] = far1[...] + far2[...] + far3[...]

    mon_energy = jnp.zeros((8, TRACES), jnp.float32)
    base_energy = jnp.zeros((8, TRACES), jnp.float32)
    for r in range(0, TIME_SAMPLES, 8):
        m = mon[pl.ds(r, 8), :]
        b = base[pl.ds(half_lags + r, 8), :]
        mon_energy = mon_energy + m * m
        base_energy = base_energy + b * b
    mon_energy = jnp.sum(mon_energy, axis=0, keepdims=True)
    base_energy = jnp.sum(base_energy, axis=0, keepdims=True)
    factor = NWIN / jnp.sqrt(mon_energy * base_energy + EPS)
    sub = lax.broadcasted_iota(jnp.int32, (8, TRACES), 0)
    width = TIME_SAMPLES // NWIN
    for lag in range(LAGS):
        level = []
        for w in range(NWIN):
            acc = None
            for r in range(w * width, (w + 1) * width, 8):
                term = mon[pl.ds(r, 8), :] * base[pl.ds(r + lag, 8), :]
                acc = term if acc is None else acc + term
            level.append(acc)
        level = [pair_sum(level[w], level[w + 4], 4, sub < 4) for w in range(4)]
        level = [pair_sum(level[w], level[w + 2], 2, (sub & 2) == 0) for w in range(2)]
        row = pair_sum(level[0], level[1], 1, (sub & 1) == 0)
        result[pl.ds(lag * 8, 8), :] = row * factor
    out[...] = result[...].T.reshape(ROWS, COLS, LAGS * NWIN)


def vmem(n):
    return [pl.BlockSpec(memory_space=pltpu.VMEM)] * n


def attributes(kernel, name, *args):
    return pl.pallas_call(
        kernel,
        out_shape=(
            jax.ShapeDtypeStruct((ROWS, COLS, TIME_SAMPLES), jnp.float32),
            jax.ShapeDtypeStruct((TIME_SAMPLES, TRACES), jnp.float32),
        ),
        in_specs=vmem(len(args)),
        out_specs=tuple(vmem(2)),
        scratch_shapes=[
            pltpu.VMEM((ROWS + 2, COLS + 8, TIME_SAMPLES), jnp.float32),
            pltpu.VMEM((9, TIME_SAMPLES + 2 * PAD, TRACES), jnp.float32),
            pltpu.VMEM((6, TIME_SAMPLES + 16, TRACES), jnp.float32),
            pltpu.VMEM((3, TIME_SAMPLES + 8, TRACES), jnp.float32),
            pltpu.VMEM((TIME_SAMPLES, TRACES), jnp.float32),
        ],
        compiler_params=pltpu.CompilerParams(vmem_limit_bytes=16 << 20),
        name=name,
    )(*args)


def correlate(mon, held, far):
    return pl.pallas_call(
        correl_kernel,
        out_shape=jax.ShapeDtypeStruct((ROWS, COLS, LAGS * NWIN), jnp.float32),
        in_specs=vmem(5),
        out_specs=pl.BlockSpec(memory_space=pltpu.VMEM),
        scratch_shapes=[
            pltpu.VMEM((TIME_SAMPLES + LAGS - 1, TRACES), jnp.float32),
            pltpu.VMEM((LAGS * NWIN, TRACES), jnp.float32),
        ],
        compiler_params=pltpu.CompilerParams(vmem_limit_bytes=16 << 20),
        name="correlate",
    )(mon, held, *far)


def pair_sends(first, last, axis):
    odd = lax.rem(lax.axis_index(axis), 2) == 1
    return jnp.where(odd, first, last), jnp.where(odd, last, first)


def swap(sends, axis, planes, rounds):
    count = lax.axis_size(axis)
    out = []
    for n, starts in enumerate(rounds):
        low = [(v * count + i, v * count + i + 1) for v in planes for i in starts]
        out.append(lax.ppermute(sends[n], ("vintage", axis), low + [(b, a) for a, b in low]))
    return out


def edge_columns(ends, rows):
    odd = lax.rem(lax.axis_index("inline"), 2) == 1
    row_a, row_b = rows[0] + rows[2], rows[1]
    above, below = jnp.where(odd, row_a, row_b), jnp.where(odd, row_b, row_a)
    first, last = (
        jnp.concatenate([above[:, j:j + 1], end, below[:, j:j + 1]], axis=0)
        for j, end in zip((0, COLS - 1), ends)
    )
    return pair_sends(first, last, "xline")


def per_device(amplitude, inline_slope, crossline_slope):
    tile = amplitude[0]
    dips = (inline_slope.reshape(1, TRACES), crossline_slope.reshape(1, TRACES))
    others = range(1, lax.axis_size("vintage"))
    along, across = ((0,), (1,), (2,)), ((0, 2, 4, 6), (1, 3, 5))
    sends = pair_sends(tile[:1], tile[-1:], "inline")
    outer = jnp.where(lax.axis_index("inline") == lax.axis_size("inline") - 1, tile[:1], tile[-1:])
    sends = (*sends, outer)
    rows = swap(sends, "inline", [0], along)
    gated = lax.optimization_barrier((sends[1], sends[2], sends[0], tile[:, :1], tile[:, -1:]))
    ends, sends = gated[3:], (gated[2], gated[0], gated[1])
    cols = swap(edge_columns(ends, rows), "xline", [0], across)
    semb0, attr0 = attributes(first_kernel, "head", tile, *[rows[n] for n in (0, 1, 2)], *cols[::-1], *dips)
    got = [lax.ppermute(attr0, "vintage", [(0, k)]) for k in (12, 4, 8)]
    rows = swap(sends, "inline", others, along)
    cols = edge_columns(ends, rows)
    cols = swap(lax.optimization_barrier((*cols, attr0))[:2], "xline", others, across)
    semb, attr = attributes(later_kernel, "tail", tile, *[rows[n] for n in (0, 1, 2)], *cols, *dips, semb0, attr0)
    got = lax.optimization_barrier((*got, attr))[:3]
    held = jnp.where(lax.axis_index("vintage") == 0, attr0, got[0] + got[1] + got[2])
    far = [lax.ppermute(held, "vintage", [(s, s + k) for s in HOLDERS]) for k in (1, 2, 3)]
    correl = correlate(attr, held, far)
    return (semb[None], correl[None])


def solution(mesh):
    return jax.shard_map(
        per_device,
        mesh=mesh,
        in_specs=(
            P("vintage", "inline", "xline", None),
            P("vintage", "inline", "xline"),
            P("vintage", "inline", "xline"),
        ),
        out_specs=(P("vintage", "inline", "xline", None), P("vintage", "inline", "xline", None)),
        check_vma=False,
    )
```

```python
import functools

import jax
import jax.numpy as jnp
from jax import lax
from jax.experimental import pallas as pl
from jax.experimental.pallas import tpu as pltpu
from jax.sharding import PartitionSpec as P

TIME_SAMPLES = 256
MAX_DIP_STEP = 2
RT = 4
LAGS = 33
NWIN = 8
EPS = 1e-06

FANOUT = {0: (8, 2, 14), 1: (9, 3, 15), 4: (6, 7, 5), 12: (10, 11, 13)}
ROWS = 8
COLS = 16
TRACES = ROWS * COLS
PAD = 16
STEPS = (-1, 0, 1)


def steered(ref, lead, row, count, sign, dip):
    out = ref[lead, pl.ds(row, count), :]
    for k in range(-MAX_DIP_STEP, MAX_DIP_STEP + 1):
        if k:
            out = jnp.where(dip == k, ref[lead, pl.ds(row + sign * k, count), :], out)
    return out


def first_kernel(*refs):
    @pl.when(lax.axis_index("vintage") == 0)
    def _():
        attr_body(*refs[:4], refs[5], refs[4], *refs[6:])


def later_kernel(*refs):
    ins, semb_first, attr_first, semb_out, attr_out = refs[:8], refs[8], refs[9], refs[10], refs[11]
    head = lax.axis_index("vintage") == 0

    @pl.when(head)
    def _():
        semb_out[...] = semb_first[...]
        attr_out[...] = attr_first[...]

    @pl.when(jnp.logical_not(head))
    def _():
        attr_body(*ins, *refs[10:])


def attr_body(tile, row_01, row_12, row_23, col_a, col_b, dip_il, dip_xl, semb_out, attr_out,
              rim, moved, inner, sums, three):
    odd_row = lax.rem(lax.axis_index("inline"), 2) == 1
    odd_col = lax.rem(lax.axis_index("xline"), 2) == 1
    rim[1:ROWS + 1, 1:COLS + 1, :] = tile[...]
    row_a, row_b = row_01[0] + row_23[0], row_12[0]
    rim[0, 1:COLS + 1, :] = jnp.where(odd_row, row_a, row_b)
    rim[ROWS + 1, 1:COLS + 1, :] = jnp.where(odd_row, row_b, row_a)
    rim[:, 0:1, :] = jnp.where(odd_col, col_a[...], col_b[...])
    rim[:, COLS + 1:COLS + 2, :] = jnp.where(odd_col, col_b[...], col_a[...])
    zeros = jnp.zeros((PAD, TRACES), jnp.float32)
    for a in STEPS:
        for b in STEPS:
            n = 3 * (a + 1) + b + 1
            block = rim[1 + a:1 + a + ROWS, 1 + b:1 + b + COLS, :].reshape(TRACES, TIME_SAMPLES)
            moved[n, 0:PAD, :] = zeros
            moved[n, PAD + TIME_SAMPLES:, :] = zeros
            moved[n, PAD:PAD + TIME_SAMPLES, :] = block.T
    q = jnp.broadcast_to(dip_xl[...], (8, TRACES))
    p = jnp.broadcast_to(dip_il[...], (8, TRACES))
    for r in range(0, TIME_SAMPLES + 16, 8):
        for a in STEPS:
            n = 3 * (a + 1) + 1
            mid = moved[n, pl.ds(r + 8, 8), :]
            lo = steered(moved, n - 1, r + 8, 8, -1, q)
            hi = steered(moved, n + 1, r + 8, 8, 1, q)
            inner[2 * (a + 1), pl.ds(r, 8), :] = lo + mid + hi
            inner[2 * (a + 1) + 1, pl.ds(r, 8), :] = lo * lo + mid * mid + hi * hi
    for r in range(0, TIME_SAMPLES + 8, 8):
        total = []
        for part in (0, 1):
            total.append(
                inner[2 + part, pl.ds(r + 4, 8), :]
                + steered(inner, part, r + 4, 8, -1, p)
                + steered(inner, 4 + part, r + 4, 8, 1, p)
            )
        sums[0, pl.ds(r, 8), :] = total[0]
        sums[1, pl.ds(r, 8), :] = total[0] * total[0]
        sums[2, pl.ds(r, 8), :] = total[1]
    for r in range(0, TIME_SAMPLES, 8):
        numer = sums[1, pl.ds(r, 8), :]
        denom = sums[2, pl.ds(r, 8), :]
        for s in range(1, 2 * RT + 1):
            numer = numer + sums[1, pl.ds(r + s, 8), :]
            denom = denom + sums[2, pl.ds(r + s, 8), :]
        semb = numer / (9.0 * denom + EPS)
        three[pl.ds(r, 8), :] = semb
        attr_out[pl.ds(r, 8), :] = semb * sums[0, pl.ds(r + RT, 8), :] * (1.0 / 9.0)
    semb_out[...] = three[...].T.reshape(ROWS, COLS, TIME_SAMPLES)


def pair_sum(x, y, half, low):
    return jnp.where(low, x, pltpu.roll(y, half, 0)) + jnp.where(low, pltpu.roll(x, 8 - half, 0), y)


def correl_kernel(mon, held, far3, far2, far1, out, base, result):
    half_lags = LAGS // 2
    place = lax.axis_index("vintage")
    holder = functools.reduce(jnp.logical_or, [place == v for v in FANOUT])
    zeros = jnp.zeros((half_lags, TRACES), jnp.float32)
    base[0:half_lags, :] = zeros
    base[half_lags + TIME_SAMPLES:, :] = zeros

    @pl.when(holder)
    def _():
        base[half_lags:half_lags + TIME_SAMPLES, :] = held[...]

    @pl.when(jnp.logical_not(holder))
    def _():
        base[half_lags:half_lags + TIME_SAMPLES, :] = far1[...] + far2[...] + far3[...]

    mon_energy = jnp.zeros((8, TRACES), jnp.float32)
    base_energy = jnp.zeros((8, TRACES), jnp.float32)
    for r in range(0, TIME_SAMPLES, 8):
        m = mon[pl.ds(r, 8), :]
        b = base[pl.ds(half_lags + r, 8), :]
        mon_energy = mon_energy + m * m
        base_energy = base_energy + b * b
    mon_energy = jnp.sum(mon_energy, axis=0, keepdims=True)
    base_energy = jnp.sum(base_energy, axis=0, keepdims=True)
    factor = NWIN / jnp.sqrt(mon_energy * base_energy + EPS)
    sub = lax.broadcasted_iota(jnp.int32, (8, TRACES), 0)
    width = TIME_SAMPLES // NWIN
    for lag in range(LAGS):
        level = []
        for w in range(NWIN):
            acc = None
            for r in range(w * width, (w + 1) * width, 8):
                term = mon[pl.ds(r, 8), :] * base[pl.ds(r + lag, 8), :]
                acc = term if acc is None else acc + term
            level.append(acc)
        level = [pair_sum(level[w], level[w + 4], 4, sub < 4) for w in range(4)]
        level = [pair_sum(level[w], level[w + 2], 2, (sub & 2) == 0) for w in range(2)]
        row = pair_sum(level[0], level[1], 1, (sub & 1) == 0)
        result[pl.ds(lag * 8, 8), :] = row * factor
    out[...] = result[...].T.reshape(ROWS, COLS, LAGS * NWIN)


def vmem(n):
    return [pl.BlockSpec(memory_space=pltpu.VMEM)] * n


def attributes(kernel, name, *args):
    return pl.pallas_call(
        kernel,
        out_shape=(
            jax.ShapeDtypeStruct((ROWS, COLS, TIME_SAMPLES), jnp.float32),
            jax.ShapeDtypeStruct((TIME_SAMPLES, TRACES), jnp.float32),
        ),
        in_specs=vmem(len(args)),
        out_specs=tuple(vmem(2)),
        scratch_shapes=[
            pltpu.VMEM((ROWS + 2, COLS + 8, TIME_SAMPLES), jnp.float32),
            pltpu.VMEM((9, TIME_SAMPLES + 2 * PAD, TRACES), jnp.float32),
            pltpu.VMEM((6, TIME_SAMPLES + 16, TRACES), jnp.float32),
            pltpu.VMEM((3, TIME_SAMPLES + 8, TRACES), jnp.float32),
            pltpu.VMEM((TIME_SAMPLES, TRACES), jnp.float32),
        ],
        compiler_params=pltpu.CompilerParams(vmem_limit_bytes=16 << 20),
        name=name,
    )(*args)


def correlate(mon, held, far):
    return pl.pallas_call(
        correl_kernel,
        out_shape=jax.ShapeDtypeStruct((ROWS, COLS, LAGS * NWIN), jnp.float32),
        in_specs=vmem(5),
        out_specs=pl.BlockSpec(memory_space=pltpu.VMEM),
        scratch_shapes=[
            pltpu.VMEM((TIME_SAMPLES + LAGS - 1, TRACES), jnp.float32),
            pltpu.VMEM((LAGS * NWIN, TRACES), jnp.float32),
        ],
        compiler_params=pltpu.CompilerParams(vmem_limit_bytes=16 << 20),
        name="correlate",
    )(mon, held, *far)


def pair_sends(first, last, axis):
    odd = lax.rem(lax.axis_index(axis), 2) == 1
    return jnp.where(odd, first, last), jnp.where(odd, last, first)


def swap(sends, axis, planes, rounds):
    count = lax.axis_size(axis)
    out = []
    for n, starts in enumerate(rounds):
        low = [(v * count + i, v * count + i + 1) for v in planes for i in starts]
        out.append(lax.ppermute(sends[n], ("vintage", axis), low + [(b, a) for a, b in low]))
    return out


def edge_columns(ends, rows):
    odd = lax.rem(lax.axis_index("inline"), 2) == 1
    row_a, row_b = rows[0] + rows[2], rows[1]
    above, below = jnp.where(odd, row_a, row_b), jnp.where(odd, row_b, row_a)
    first, last = (
        jnp.concatenate([above[:, j:j + 1], end, below[:, j:j + 1]], axis=0)
        for j, end in zip((0, COLS - 1), ends)
    )
    return pair_sends(first, last, "xline")


def per_device(amplitude, inline_slope, crossline_slope):
    tile = amplitude[0]
    dips = (inline_slope.reshape(1, TRACES), crossline_slope.reshape(1, TRACES))
    others = range(1, lax.axis_size("vintage"))
    along, across = ((0,), (1,), (2,)), ((0, 2, 4, 6), (1, 3, 5))
    sends = pair_sends(tile[:1], tile[-1:], "inline")
    outer = jnp.where(lax.axis_index("inline") == lax.axis_size("inline") - 1, tile[:1], tile[-1:])
    sends = (*sends, outer)
    rows = swap(sends, "inline", [0], along)
    gated = lax.optimization_barrier((sends[1], sends[2], sends[0], tile[:, :1], tile[:, -1:]))
    ends, sends = gated[3:], (gated[2], gated[0], gated[1])
    cols = swap(edge_columns(ends, rows), "xline", [0], across)
    semb0, attr0 = attributes(first_kernel, "head", tile, *[rows[n] for n in (0, 1, 2)], *cols[::-1], *dips)
    got = [lax.ppermute(attr0, "vintage", [(0, k)]) for k in (1, 12, 4)]
    rows = swap(sends, "inline", others, along)
    cols = edge_columns(ends, rows)
    cols = swap(lax.optimization_barrier((*cols, attr0))[:2], "xline", others, across)
    joined = lax.optimization_barrier((*got, *cols))
    got, cols = joined[:3], joined[3:]
    semb, attr = attributes(later_kernel, "tail", tile, *[rows[n] for n in (0, 1, 2)], *cols, *dips, semb0, attr0)
    held = jnp.where(lax.axis_index("vintage") == 0, attr0, got[0] + got[1] + got[2])
    far = [lax.ppermute(held, "vintage", [(s, to[n]) for s, to in FANOUT.items()]) for n in (2, 1, 0)]
    correl = correlate(attr, held, far)
    return (semb[None], correl[None])


def solution(mesh):
    return jax.shard_map(
        per_device,
        mesh=mesh,
        in_specs=(
            P("vintage", "inline", "xline", None),
            P("vintage", "inline", "xline"),
            P("vintage", "inline", "xline"),
        ),
        out_specs=(P("vintage", "inline", "xline", None), P("vintage", "inline", "xline", None)),
        check_vma=False,
    )
```

```python
import functools

import jax
import jax.numpy as jnp
from jax import lax
from jax.experimental import pallas as pl
from jax.experimental.pallas import tpu as pltpu
from jax.sharding import PartitionSpec as P

TIME_SAMPLES = 256
MAX_DIP_STEP = 2
RT = 4
LAGS = 33
NWIN = 8
EPS = 1e-06

FANOUT = {0: (8, 4, 12), 1: (9, 5, 13), 2: (6, 7, 3), 14: (10, 11, 15)}
ROWS = 8
COLS = 16
TRACES = ROWS * COLS
PAD = 16
STEPS = (-1, 0, 1)


def steered(ref, lead, row, count, sign, dip):
    out = ref[lead, pl.ds(row, count), :]
    for k in range(-MAX_DIP_STEP, MAX_DIP_STEP + 1):
        if k:
            out = jnp.where(dip == k, ref[lead, pl.ds(row + sign * k, count), :], out)
    return out


def is_head(place):
    return functools.reduce(jnp.logical_or, [place == v for v in FANOUT])


def head_kernel(*refs):
    @pl.when(is_head(lax.axis_index("vintage")))
    def _():
        attr_body(*refs[:4], refs[5], refs[4], *refs[6:])


def tail_kernel(*refs):
    ins, semb_head, attr_head, semb_out, attr_out = refs[:8], refs[8], refs[9], refs[10], refs[11]
    head = is_head(lax.axis_index("vintage"))

    @pl.when(head)
    def _():
        semb_out[...] = semb_head[...]
        attr_out[...] = attr_head[...]

    @pl.when(jnp.logical_not(head))
    def _():
        attr_body(*ins, *refs[10:])


def attr_body(tile, row_12, row_23, row_01, col_a, col_b, dip_il, dip_xl, semb_out, attr_out,
              rim, moved, inner, sums, three):
    odd_row = lax.rem(lax.axis_index("inline"), 2) == 1
    odd_col = lax.rem(lax.axis_index("xline"), 2) == 1
    rim[1:ROWS + 1, 1:COLS + 1, :] = tile[...]
    row_a, row_b = row_01[0] + row_23[0], row_12[0]
    rim[0, 1:COLS + 1, :] = jnp.where(odd_row, row_a, row_b)
    rim[ROWS + 1, 1:COLS + 1, :] = jnp.where(odd_row, row_b, row_a)
    rim[:, 0:1, :] = jnp.where(odd_col, col_a[...], col_b[...])
    rim[:, COLS + 1:COLS + 2, :] = jnp.where(odd_col, col_b[...], col_a[...])
    zeros = jnp.zeros((PAD, TRACES), jnp.float32)
    for a in STEPS:
        for b in STEPS:
            n = 3 * (a + 1) + b + 1
            block = rim[1 + a:1 + a + ROWS, 1 + b:1 + b + COLS, :].reshape(TRACES, TIME_SAMPLES)
            moved[n, 0:PAD, :] = zeros
            moved[n, PAD + TIME_SAMPLES:, :] = zeros
            moved[n, PAD:PAD + TIME_SAMPLES, :] = block.T
    q = jnp.broadcast_to(dip_xl[...], (8, TRACES))
    p = jnp.broadcast_to(dip_il[...], (8, TRACES))
    for r in range(0, TIME_SAMPLES + 16, 8):
        for a in STEPS:
            n = 3 * (a + 1) + 1
            mid = moved[n, pl.ds(r + 8, 8), :]
            lo = steered(moved, n - 1, r + 8, 8, -1, q)
            hi = steered(moved, n + 1, r + 8, 8, 1, q)
            inner[2 * (a + 1), pl.ds(r, 8), :] = lo + mid + hi
            inner[2 * (a + 1) + 1, pl.ds(r, 8), :] = lo * lo + mid * mid + hi * hi
    for r in range(0, TIME_SAMPLES + 8, 8):
        total = []
        for part in (0, 1):
            total.append(
                inner[2 + part, pl.ds(r + 4, 8), :]
                + steered(inner, part, r + 4, 8, -1, p)
                + steered(inner, 4 + part, r + 4, 8, 1, p)
            )
        sums[0, pl.ds(r, 8), :] = total[0]
        sums[1, pl.ds(r, 8), :] = total[0] * total[0]
        sums[2, pl.ds(r, 8), :] = total[1]
    for r in range(0, TIME_SAMPLES, 8):
        numer = sums[1, pl.ds(r, 8), :]
        denom = sums[2, pl.ds(r, 8), :]
        for s in range(1, 2 * RT + 1):
            numer = numer + sums[1, pl.ds(r + s, 8), :]
            denom = denom + sums[2, pl.ds(r + s, 8), :]
        semb = numer / (9.0 * denom + EPS)
        three[pl.ds(r, 8), :] = semb
        attr_out[pl.ds(r, 8), :] = semb * sums[0, pl.ds(r + RT, 8), :] * (1.0 / 9.0)
    semb_out[...] = three[...].T.reshape(ROWS, COLS, TIME_SAMPLES)


def pair_sum(x, y, half, low):
    return jnp.where(low, x, pltpu.roll(y, half, 0)) + jnp.where(low, pltpu.roll(x, 8 - half, 0), y)


def correl_kernel(mon, held, far3, far2, far1, out, base, result):
    half_lags = LAGS // 2
    holder = is_head(lax.axis_index("vintage"))
    zeros = jnp.zeros((half_lags, TRACES), jnp.float32)
    base[0:half_lags, :] = zeros
    base[half_lags + TIME_SAMPLES:, :] = zeros

    @pl.when(holder)
    def _():
        base[half_lags:half_lags + TIME_SAMPLES, :] = held[...]

    @pl.when(jnp.logical_not(holder))
    def _():
        base[half_lags:half_lags + TIME_SAMPLES, :] = far1[...] + far2[...] + far3[...]

    mon_energy = jnp.zeros((8, TRACES), jnp.float32)
    base_energy = jnp.zeros((8, TRACES), jnp.float32)
    for r in range(0, TIME_SAMPLES, 8):
        m = mon[pl.ds(r, 8), :]
        b = base[pl.ds(half_lags + r, 8), :]
        mon_energy = mon_energy + m * m
        base_energy = base_energy + b * b
    mon_energy = jnp.sum(mon_energy, axis=0, keepdims=True)
    base_energy = jnp.sum(base_energy, axis=0, keepdims=True)
    factor = NWIN / jnp.sqrt(mon_energy * base_energy + EPS)
    sub = lax.broadcasted_iota(jnp.int32, (8, TRACES), 0)
    width = TIME_SAMPLES // NWIN
    for lag in range(LAGS):
        level = []
        for w in range(NWIN):
            acc = None
            for r in range(w * width, (w + 1) * width, 8):
                term = mon[pl.ds(r, 8), :] * base[pl.ds(r + lag, 8), :]
                acc = term if acc is None else acc + term
            level.append(acc)
        level = [pair_sum(level[w], level[w + 4], 4, sub < 4) for w in range(4)]
        level = [pair_sum(level[w], level[w + 2], 2, (sub & 2) == 0) for w in range(2)]
        row = pair_sum(level[0], level[1], 1, (sub & 1) == 0)
        result[pl.ds(lag * 8, 8), :] = row * factor
    out[...] = result[...].T.reshape(ROWS, COLS, LAGS * NWIN)


def vmem(n):
    return [pl.BlockSpec(memory_space=pltpu.VMEM)] * n


def attributes(kernel, name, *args):
    return pl.pallas_call(
        kernel,
        out_shape=(
            jax.ShapeDtypeStruct((ROWS, COLS, TIME_SAMPLES), jnp.float32),
            jax.ShapeDtypeStruct((TIME_SAMPLES, TRACES), jnp.float32),
        ),
        in_specs=vmem(len(args)),
        out_specs=tuple(vmem(2)),
        scratch_shapes=[
            pltpu.VMEM((ROWS + 2, COLS + 8, TIME_SAMPLES), jnp.float32),
            pltpu.VMEM((9, TIME_SAMPLES + 2 * PAD, TRACES), jnp.float32),
            pltpu.VMEM((6, TIME_SAMPLES + 16, TRACES), jnp.float32),
            pltpu.VMEM((3, TIME_SAMPLES + 8, TRACES), jnp.float32),
            pltpu.VMEM((TIME_SAMPLES, TRACES), jnp.float32),
        ],
        compiler_params=pltpu.CompilerParams(vmem_limit_bytes=16 << 20),
        name=name,
    )(*args)


def correlate(mon, held, far):
    return pl.pallas_call(
        correl_kernel,
        out_shape=jax.ShapeDtypeStruct((ROWS, COLS, LAGS * NWIN), jnp.float32),
        in_specs=vmem(5),
        out_specs=pl.BlockSpec(memory_space=pltpu.VMEM),
        scratch_shapes=[
            pltpu.VMEM((TIME_SAMPLES + LAGS - 1, TRACES), jnp.float32),
            pltpu.VMEM((LAGS * NWIN, TRACES), jnp.float32),
        ],
        compiler_params=pltpu.CompilerParams(vmem_limit_bytes=16 << 20),
        name="correlate",
    )(mon, held, *far)


def pair_sends(first, last, axis):
    odd = lax.rem(lax.axis_index(axis), 2) == 1
    return jnp.where(odd, first, last), jnp.where(odd, last, first)


def swap(sends, axis, planes, rounds):
    count = lax.axis_size(axis)
    out = []
    for n, starts in enumerate(rounds):
        low = [(v * count + i, v * count + i + 1) for v in planes for i in starts]
        out.append(lax.ppermute(sends[n], ("vintage", axis), low + [(b, a) for a, b in low]))
    return out


def edge_columns(ends, rows):
    odd = lax.rem(lax.axis_index("inline"), 2) == 1
    row_a, row_b = rows[0] + rows[2], rows[1]
    above, below = jnp.where(odd, row_a, row_b), jnp.where(odd, row_b, row_a)
    first, last = (
        jnp.concatenate([above[:, j:j + 1], end, below[:, j:j + 1]], axis=0)
        for j, end in zip((0, COLS - 1), ends)
    )
    return pair_sends(first, last, "xline")


def per_device(amplitude, inline_slope, crossline_slope):
    tile = amplitude[0]
    dips = (inline_slope.reshape(1, TRACES), crossline_slope.reshape(1, TRACES))
    vintages = lax.axis_size("vintage")
    others = [v for v in range(vintages) if v not in FANOUT]
    along, across = ((0,), (1,), (2,)), ((0, 2, 4, 6), (1, 3, 5))
    sends = pair_sends(tile[:1], tile[-1:], "inline")
    outer = jnp.where(lax.axis_index("inline") == lax.axis_size("inline") - 1, tile[:1], tile[-1:])
    rows = swap((*sends, outer), "inline", range(vintages), along)
    sends = edge_columns((tile[:, :1], tile[:, -1:]), rows)
    cols = swap(sends, "xline", FANOUT, across)
    semb0, attr0 = attributes(head_kernel, "head", tile, *[rows[n] for n in (1, 2, 0)], *cols[::-1], *dips)
    got = [lax.ppermute(attr0, "vintage", [(0, k)]) for k in (14, 2, 1)]
    held = jnp.where(lax.axis_index("vintage") == 0, attr0, got[0] + got[1] + got[2])
    far = [lax.ppermute(held, "vintage", [(s, to[n]) for s, to in FANOUT.items()]) for n in (2, 1, 0)]
    cols = swap(lax.optimization_barrier((*sends, held))[:2], "xline", others, across)
    semb, attr = attributes(tail_kernel, "tail", tile, *[rows[n] for n in (1, 2, 0)], *cols, *dips, semb0, attr0)
    correl = correlate(attr, held, far)
    return (semb[None], correl[None])


def solution(mesh):
    return jax.shard_map(
        per_device,
        mesh=mesh,
        in_specs=(
            P("vintage", "inline", "xline", None),
            P("vintage", "inline", "xline"),
            P("vintage", "inline", "xline"),
        ),
        out_specs=(P("vintage", "inline", "xline", None), P("vintage", "inline", "xline", None)),
        check_vma=False,
    )
```

```python
import jax
import jax.numpy as jnp
from jax import lax
from jax.experimental import pallas as pl
from jax.experimental.pallas import tpu as pltpu
from jax.sharding import PartitionSpec as P

TIME_SAMPLES = 256
MAX_DIP_STEP = 2
RT = 4
LAGS = 33
NWIN = 8
EPS = 1e-06

FANOUT = {0: (3, 2, 1), 4: (7, 6, 5), 8: (11, 10, 9), 12: (15, 14, 13)}
ROWS = 8
COLS = 16
TRACES = ROWS * COLS
PAD = 16
STEPS = (-1, 0, 1)


def steered(ref, lead, row, count, sign, dip):
    out = ref[lead, pl.ds(row, count), :]
    for k in range(-MAX_DIP_STEP, MAX_DIP_STEP + 1):
        if k:
            out = jnp.where(dip == k, ref[lead, pl.ds(row + sign * k, count), :], out)
    return out


def head_kernel(*refs):
    @pl.when(lax.axis_index("vintage") == 0)
    def _():
        attr_body(*refs[:4], refs[5], refs[4], *refs[6:])


def tail_kernel(*refs):
    ins, semb_head, attr_head, semb_out, attr_out = refs[:8], refs[8], refs[9], refs[10], refs[11]
    head = lax.axis_index("vintage") == 0

    @pl.when(head)
    def _():
        semb_out[...] = semb_head[...]
        attr_out[...] = attr_head[...]

    @pl.when(jnp.logical_not(head))
    def _():
        attr_body(*ins, *refs[10:])


def attr_body(tile, row_12, row_23, row_01, col_a, col_b, dip_il, dip_xl, semb_out, attr_out,
              rim, moved, inner, sums, three):
    odd_row = lax.rem(lax.axis_index("inline"), 2) == 1
    odd_col = lax.rem(lax.axis_index("xline"), 2) == 1
    rim[1:ROWS + 1, 1:COLS + 1, :] = tile[...]
    row_a, row_b = row_01[0] + row_23[0], row_12[0]
    rim[0, 1:COLS + 1, :] = jnp.where(odd_row, row_a, row_b)
    rim[ROWS + 1, 1:COLS + 1, :] = jnp.where(odd_row, row_b, row_a)
    rim[:, 0:1, :] = jnp.where(odd_col, col_a[...], col_b[...])
    rim[:, COLS + 1:COLS + 2, :] = jnp.where(odd_col, col_b[...], col_a[...])
    zeros = jnp.zeros((PAD, TRACES), jnp.float32)
    for a in STEPS:
        for b in STEPS:
            n = 3 * (a + 1) + b + 1
            block = rim[1 + a:1 + a + ROWS, 1 + b:1 + b + COLS, :].reshape(TRACES, TIME_SAMPLES)
            moved[n, 0:PAD, :] = zeros
            moved[n, PAD + TIME_SAMPLES:, :] = zeros
            moved[n, PAD:PAD + TIME_SAMPLES, :] = block.T
    q = jnp.broadcast_to(dip_xl[...], (8, TRACES))
    p = jnp.broadcast_to(dip_il[...], (8, TRACES))
    for r in range(0, TIME_SAMPLES + 16, 8):
        for a in STEPS:
            n = 3 * (a + 1) + 1
            mid = moved[n, pl.ds(r + 8, 8), :]
            lo = steered(moved, n - 1, r + 8, 8, -1, q)
            hi = steered(moved, n + 1, r + 8, 8, 1, q)
            inner[2 * (a + 1), pl.ds(r, 8), :] = lo + mid + hi
            inner[2 * (a + 1) + 1, pl.ds(r, 8), :] = lo * lo + mid * mid + hi * hi
    for r in range(0, TIME_SAMPLES + 8, 8):
        total = []
        for part in (0, 1):
            total.append(
                inner[2 + part, pl.ds(r + 4, 8), :]
                + steered(inner, part, r + 4, 8, -1, p)
                + steered(inner, 4 + part, r + 4, 8, 1, p)
            )
        sums[0, pl.ds(r, 8), :] = total[0]
        sums[1, pl.ds(r, 8), :] = total[0] * total[0]
        sums[2, pl.ds(r, 8), :] = total[1]
    for r in range(0, TIME_SAMPLES, 8):
        numer = sums[1, pl.ds(r, 8), :]
        denom = sums[2, pl.ds(r, 8), :]
        for s in range(1, 2 * RT + 1):
            numer = numer + sums[1, pl.ds(r + s, 8), :]
            denom = denom + sums[2, pl.ds(r + s, 8), :]
        semb = numer / (9.0 * denom + EPS)
        three[pl.ds(r, 8), :] = semb
        attr_out[pl.ds(r, 8), :] = semb * sums[0, pl.ds(r + RT, 8), :] * (1.0 / 9.0)
    semb_out[...] = three[...].T.reshape(ROWS, COLS, TIME_SAMPLES)


def pair_sum(x, y, half, low):
    return jnp.where(low, x, pltpu.roll(y, half, 0)) + jnp.where(low, pltpu.roll(x, 8 - half, 0), y)


def correl_kernel(mon, held, far3, far2, far1, out, base, result):
    half_lags = LAGS // 2
    holder = lax.rem(lax.axis_index("vintage"), 4) == 0
    zeros = jnp.zeros((half_lags, TRACES), jnp.float32)
    base[0:half_lags, :] = zeros
    base[half_lags + TIME_SAMPLES:, :] = zeros

    @pl.when(holder)
    def _():
        base[half_lags:half_lags + TIME_SAMPLES, :] = held[...]

    @pl.when(jnp.logical_not(holder))
    def _():
        base[half_lags:half_lags + TIME_SAMPLES, :] = far1[...] + far2[...] + far3[...]

    mon_energy = jnp.zeros((8, TRACES), jnp.float32)
    base_energy = jnp.zeros((8, TRACES), jnp.float32)
    for r in range(0, TIME_SAMPLES, 8):
        m = mon[pl.ds(r, 8), :]
        b = base[pl.ds(half_lags + r, 8), :]
        mon_energy = mon_energy + m * m
        base_energy = base_energy + b * b
    mon_energy = jnp.sum(mon_energy, axis=0, keepdims=True)
    base_energy = jnp.sum(base_energy, axis=0, keepdims=True)
    factor = NWIN / jnp.sqrt(mon_energy * base_energy + EPS)
    sub = lax.broadcasted_iota(jnp.int32, (8, TRACES), 0)
    width = TIME_SAMPLES // NWIN
    for lag in range(LAGS):
        level = []
        for w in range(NWIN):
            acc = None
            for r in range(w * width, (w + 1) * width, 8):
                term = mon[pl.ds(r, 8), :] * base[pl.ds(r + lag, 8), :]
                acc = term if acc is None else acc + term
            level.append(acc)
        level = [pair_sum(level[w], level[w + 4], 4, sub < 4) for w in range(4)]
        level = [pair_sum(level[w], level[w + 2], 2, (sub & 2) == 0) for w in range(2)]
        row = pair_sum(level[0], level[1], 1, (sub & 1) == 0)
        result[pl.ds(lag * 8, 8), :] = row * factor
    out[...] = result[...].T.reshape(ROWS, COLS, LAGS * NWIN)


def vmem(n):
    return [pl.BlockSpec(memory_space=pltpu.VMEM)] * n


def attributes(kernel, name, *args):
    return pl.pallas_call(
        kernel,
        out_shape=(
            jax.ShapeDtypeStruct((ROWS, COLS, TIME_SAMPLES), jnp.float32),
            jax.ShapeDtypeStruct((TIME_SAMPLES, TRACES), jnp.float32),
        ),
        in_specs=vmem(len(args)),
        out_specs=tuple(vmem(2)),
        scratch_shapes=[
            pltpu.VMEM((ROWS + 2, COLS + 8, TIME_SAMPLES), jnp.float32),
            pltpu.VMEM((9, TIME_SAMPLES + 2 * PAD, TRACES), jnp.float32),
            pltpu.VMEM((6, TIME_SAMPLES + 16, TRACES), jnp.float32),
            pltpu.VMEM((3, TIME_SAMPLES + 8, TRACES), jnp.float32),
            pltpu.VMEM((TIME_SAMPLES, TRACES), jnp.float32),
        ],
        compiler_params=pltpu.CompilerParams(vmem_limit_bytes=16 << 20),
        name=name,
    )(*args)


def correlate(mon, held, far):
    return pl.pallas_call(
        correl_kernel,
        out_shape=jax.ShapeDtypeStruct((ROWS, COLS, LAGS * NWIN), jnp.float32),
        in_specs=vmem(5),
        out_specs=pl.BlockSpec(memory_space=pltpu.VMEM),
        scratch_shapes=[
            pltpu.VMEM((TIME_SAMPLES + LAGS - 1, TRACES), jnp.float32),
            pltpu.VMEM((LAGS * NWIN, TRACES), jnp.float32),
        ],
        compiler_params=pltpu.CompilerParams(vmem_limit_bytes=16 << 20),
        name="correlate",
    )(mon, held, *far)


def pair_sends(first, last, axis):
    odd = lax.rem(lax.axis_index(axis), 2) == 1
    return jnp.where(odd, first, last), jnp.where(odd, last, first)


def swap(sends, axis, planes, rounds):
    count = lax.axis_size(axis)
    out = []
    for n, starts in enumerate(rounds):
        low = [(v * count + i, v * count + i + 1) for v in planes for i in starts]
        out.append(lax.ppermute(sends[n], ("vintage", axis), low + [(b, a) for a, b in low]))
    return out


def edge_columns(ends, rows):
    odd = lax.rem(lax.axis_index("inline"), 2) == 1
    row_a, row_b = rows[0] + rows[2], rows[1]
    above, below = jnp.where(odd, row_a, row_b), jnp.where(odd, row_b, row_a)
    first, last = (
        jnp.concatenate([above[:, j:j + 1], end, below[:, j:j + 1]], axis=0)
        for j, end in zip((0, COLS - 1), ends)
    )
    return pair_sends(first, last, "xline")


def per_device(amplitude, inline_slope, crossline_slope):
    tile = amplitude[0]
    dips = (inline_slope.reshape(1, TRACES), crossline_slope.reshape(1, TRACES))
    vintages = lax.axis_size("vintage")
    along, across = ((0,), (1,), (2,)), ((0, 2, 4, 6), (1, 3, 5))
    sends = pair_sends(tile[:1], tile[-1:], "inline")
    outer = jnp.where(lax.axis_index("inline") == lax.axis_size("inline") - 1, tile[:1], tile[-1:])
    rows = swap((*sends, outer), "inline", range(vintages), along)
    sends = edge_columns((tile[:, :1], tile[:, -1:]), rows)
    rows = [rows[n] for n in (1, 2, 0)]
    cols = swap(sends, "xline", [0], across)
    semb0, attr0 = attributes(head_kernel, "head", tile, *rows, *cols[::-1], *dips)
    got = [lax.ppermute(attr0, "vintage", [(0, k)]) for k in (12, 4, 8)]
    cols = swap(lax.optimization_barrier((*sends, attr0))[:2], "xline", range(1, vintages), across)
    joined = lax.optimization_barrier((*got, *cols))
    got, cols = joined[:3], joined[3:]
    held = jnp.where(lax.axis_index("vintage") == 0, attr0, got[0] + got[1] + got[2])
    far = [lax.ppermute(held, "vintage", [(s, to[n]) for s, to in FANOUT.items()]) for n in (2, 1, 0)]
    semb, attr = attributes(tail_kernel, "tail", tile, *rows, *cols, *dips, semb0, attr0)
    correl = correlate(attr, held, far)
    return (semb[None], correl[None])


def solution(mesh):
    return jax.shard_map(
        per_device,
        mesh=mesh,
        in_specs=(
            P("vintage", "inline", "xline", None),
            P("vintage", "inline", "xline"),
            P("vintage", "inline", "xline"),
        ),
        out_specs=(P("vintage", "inline", "xline", None), P("vintage", "inline", "xline", None)),
        check_vma=False,
    )
```

```python
import jax
import jax.numpy as jnp
from jax import lax
from jax.experimental import pallas as pl
from jax.experimental.pallas import tpu as pltpu
from jax.sharding import PartitionSpec as P

TIME_SAMPLES = 256
MAX_DIP_STEP = 2
RT = 4
LAGS = 33
NWIN = 8
EPS = 1e-06

FANOUT = {0: (3, 2, 1), 4: (7, 6, 5), 8: (11, 10, 9), 12: (15, 14, 13)}
ROWS = 8
COLS = 16
TRACES = ROWS * COLS
PAD = 16
STEPS = (-1, 0, 1)


def steered(ref, lead, row, count, sign, dip):
    out = ref[lead, pl.ds(row, count), :]
    for k in range(-MAX_DIP_STEP, MAX_DIP_STEP + 1):
        if k:
            out = jnp.where(dip == k, ref[lead, pl.ds(row + sign * k, count), :], out)
    return out


def head_kernel(tile, row_12, row_23, row_01, cols, dip_il, dip_xl, *rest):
    @pl.when(lax.axis_index("vintage") == 0)
    def _():
        edges = cols[0:ROWS + 2], cols[ROWS + 2:]
        attr_body(tile, row_12, row_23, row_01, edges, dip_il, dip_xl, *rest)


def tail_kernel(tile, row_12, row_23, row_01, col_a, col_b, dip_il, dip_xl, semb_head, attr_head,
                semb_out, attr_out, *scratch):
    head = lax.axis_index("vintage") == 0

    @pl.when(head)
    def _():
        semb_out[...] = semb_head[...]
        attr_out[...] = attr_head[...]

    @pl.when(jnp.logical_not(head))
    def _():
        odd = lax.rem(lax.axis_index("xline"), 2) == 1
        edges = jnp.where(odd, col_a[...], col_b[...]), jnp.where(odd, col_b[...], col_a[...])
        attr_body(tile, row_12, row_23, row_01, edges, dip_il, dip_xl, semb_out, attr_out, *scratch)


def attr_body(tile, row_12, row_23, row_01, edges, dip_il, dip_xl, semb_out, attr_out,
              rim, moved, inner, sums, three):
    odd_row = lax.rem(lax.axis_index("inline"), 2) == 1
    rim[1:ROWS + 1, 1:COLS + 1, :] = tile[...]
    row_a, row_b = row_01[0] + row_23[0], row_12[0]
    rim[0, 1:COLS + 1, :] = jnp.where(odd_row, row_a, row_b)
    rim[ROWS + 1, 1:COLS + 1, :] = jnp.where(odd_row, row_b, row_a)
    rim[:, 0:1, :] = edges[0]
    rim[:, COLS + 1:COLS + 2, :] = edges[1]
    zeros = jnp.zeros((PAD, TRACES), jnp.float32)
    for a in STEPS:
        for b in STEPS:
            n = 3 * (a + 1) + b + 1
            block = rim[1 + a:1 + a + ROWS, 1 + b:1 + b + COLS, :].reshape(TRACES, TIME_SAMPLES)
            moved[n, 0:PAD, :] = zeros
            moved[n, PAD + TIME_SAMPLES:, :] = zeros
            moved[n, PAD:PAD + TIME_SAMPLES, :] = block.T
    q = jnp.broadcast_to(dip_xl[...], (8, TRACES))
    p = jnp.broadcast_to(dip_il[...], (8, TRACES))
    for r in range(0, TIME_SAMPLES + 16, 8):
        for a in STEPS:
            n = 3 * (a + 1) + 1
            mid = moved[n, pl.ds(r + 8, 8), :]
            lo = steered(moved, n - 1, r + 8, 8, -1, q)
            hi = steered(moved, n + 1, r + 8, 8, 1, q)
            inner[2 * (a + 1), pl.ds(r, 8), :] = lo + mid + hi
            inner[2 * (a + 1) + 1, pl.ds(r, 8), :] = lo * lo + mid * mid + hi * hi
    for r in range(0, TIME_SAMPLES + 8, 8):
        total = []
        for part in (0, 1):
            total.append(
                inner[2 + part, pl.ds(r + 4, 8), :]
                + steered(inner, part, r + 4, 8, -1, p)
                + steered(inner, 4 + part, r + 4, 8, 1, p)
            )
        sums[0, pl.ds(r, 8), :] = total[0]
        sums[1, pl.ds(r, 8), :] = total[0] * total[0]
        sums[2, pl.ds(r, 8), :] = total[1]
    for r in range(0, TIME_SAMPLES, 8):
        numer = sums[1, pl.ds(r, 8), :]
        denom = sums[2, pl.ds(r, 8), :]
        for s in range(1, 2 * RT + 1):
            numer = numer + sums[1, pl.ds(r + s, 8), :]
            denom = denom + sums[2, pl.ds(r + s, 8), :]
        semb = numer / (9.0 * denom + EPS)
        three[pl.ds(r, 8), :] = semb
        attr_out[pl.ds(r, 8), :] = semb * sums[0, pl.ds(r + RT, 8), :] * (1.0 / 9.0)
    semb_out[...] = three[...].T.reshape(ROWS, COLS, TIME_SAMPLES)


def pair_sum(x, y, half, low):
    return jnp.where(low, x, pltpu.roll(y, half, 0)) + jnp.where(low, pltpu.roll(x, 8 - half, 0), y)


def correl_kernel(mon, held, far3, far2, far1, out, base, result):
    half_lags = LAGS // 2
    holder = lax.rem(lax.axis_index("vintage"), 4) == 0
    zeros = jnp.zeros((half_lags, TRACES), jnp.float32)
    base[0:half_lags, :] = zeros
    base[half_lags + TIME_SAMPLES:, :] = zeros

    @pl.when(holder)
    def _():
        base[half_lags:half_lags + TIME_SAMPLES, :] = held[...]

    @pl.when(jnp.logical_not(holder))
    def _():
        base[half_lags:half_lags + TIME_SAMPLES, :] = far1[...] + far2[...] + far3[...]

    mon_energy = jnp.zeros((8, TRACES), jnp.float32)
    base_energy = jnp.zeros((8, TRACES), jnp.float32)
    for r in range(0, TIME_SAMPLES, 8):
        m = mon[pl.ds(r, 8), :]
        b = base[pl.ds(half_lags + r, 8), :]
        mon_energy = mon_energy + m * m
        base_energy = base_energy + b * b
    mon_energy = jnp.sum(mon_energy, axis=0, keepdims=True)
    base_energy = jnp.sum(base_energy, axis=0, keepdims=True)
    factor = NWIN / jnp.sqrt(mon_energy * base_energy + EPS)
    sub = lax.broadcasted_iota(jnp.int32, (8, TRACES), 0)
    width = TIME_SAMPLES // NWIN
    for lag in range(LAGS):
        level = []
        for w in range(NWIN):
            acc = None
            for r in range(w * width, (w + 1) * width, 8):
                term = mon[pl.ds(r, 8), :] * base[pl.ds(r + lag, 8), :]
                acc = term if acc is None else acc + term
            level.append(acc)
        level = [pair_sum(level[w], level[w + 4], 4, sub < 4) for w in range(4)]
        level = [pair_sum(level[w], level[w + 2], 2, (sub & 2) == 0) for w in range(2)]
        row = pair_sum(level[0], level[1], 1, (sub & 1) == 0)
        result[pl.ds(lag * 8, 8), :] = row * factor
    out[...] = result[...].T.reshape(ROWS, COLS, LAGS * NWIN)


def vmem(n):
    return [pl.BlockSpec(memory_space=pltpu.VMEM)] * n


def attributes(kernel, name, *args):
    return pl.pallas_call(
        kernel,
        out_shape=(
            jax.ShapeDtypeStruct((ROWS, COLS, TIME_SAMPLES), jnp.float32),
            jax.ShapeDtypeStruct((TIME_SAMPLES, TRACES), jnp.float32),
        ),
        in_specs=vmem(len(args)),
        out_specs=tuple(vmem(2)),
        scratch_shapes=[
            pltpu.VMEM((ROWS + 2, COLS + 8, TIME_SAMPLES), jnp.float32),
            pltpu.VMEM((9, TIME_SAMPLES + 2 * PAD, TRACES), jnp.float32),
            pltpu.VMEM((6, TIME_SAMPLES + 16, TRACES), jnp.float32),
            pltpu.VMEM((3, TIME_SAMPLES + 8, TRACES), jnp.float32),
            pltpu.VMEM((TIME_SAMPLES, TRACES), jnp.float32),
        ],
        compiler_params=pltpu.CompilerParams(vmem_limit_bytes=16 << 20),
        name=name,
    )(*args)


def correlate(mon, held, far):
    return pl.pallas_call(
        correl_kernel,
        out_shape=jax.ShapeDtypeStruct((ROWS, COLS, LAGS * NWIN), jnp.float32),
        in_specs=vmem(5),
        out_specs=pl.BlockSpec(memory_space=pltpu.VMEM),
        scratch_shapes=[
            pltpu.VMEM((TIME_SAMPLES + LAGS - 1, TRACES), jnp.float32),
            pltpu.VMEM((LAGS * NWIN, TRACES), jnp.float32),
        ],
        compiler_params=pltpu.CompilerParams(vmem_limit_bytes=16 << 20),
        name="correlate",
    )(mon, held, *far)


def pair_sends(first, last, axis):
    odd = lax.rem(lax.axis_index(axis), 2) == 1
    return jnp.where(odd, first, last), jnp.where(odd, last, first)


def swap(sends, axis, planes, rounds):
    count = lax.axis_size(axis)
    out = []
    for n, starts in enumerate(rounds):
        low = [(v * count + i, v * count + i + 1) for v in planes for i in starts]
        out.append(lax.ppermute(sends[n], ("vintage", axis), low + [(b, a) for a, b in low]))
    return out


def edge_columns(ends, rows):
    odd = lax.rem(lax.axis_index("inline"), 2) == 1
    row_a, row_b = rows[0] + rows[2], rows[1]
    above, below = jnp.where(odd, row_a, row_b), jnp.where(odd, row_b, row_a)
    return [
        jnp.concatenate([above[:, j:j + 1], end, below[:, j:j + 1]], axis=0)
        for j, end in zip((0, COLS - 1), ends)
    ]


def per_device(amplitude, inline_slope, crossline_slope):
    tile = amplitude[0]
    dips = (inline_slope.reshape(1, TRACES), crossline_slope.reshape(1, TRACES))
    vintages, width = lax.axis_size("vintage"), lax.axis_size("xline")
    along, across = ((0,), (1,), (2,)), ((0, 2, 4, 6), (1, 3, 5))
    sends = pair_sends(tile[:1], tile[-1:], "inline")
    outer = jnp.where(lax.axis_index("inline") == lax.axis_size("inline") - 1, tile[:1], tile[-1:])
    rows = swap((*sends, outer), "inline", range(vintages), along)
    first, last = edge_columns((tile[:, :1], tile[:, -1:]), rows)
    rows = [rows[n] for n in (1, 2, 0)]
    both = "vintage", "xline"
    left = lax.ppermute(last, both, [(x, width + x + 1) for x in range(width - 1)])
    right = lax.ppermute(first, both, [(x + 1, width + x) for x in range(width - 1)])
    cols = lax.ppermute(jnp.concatenate([left, right], axis=0), "vintage", [(1, 0)])
    semb0, attr0 = attributes(head_kernel, "head", tile, *rows, cols, *dips)
    got = [lax.ppermute(attr0, "vintage", [(0, k)]) for k in (12, 4, 8)]
    first, last = lax.optimization_barrier((first, last, attr0))[:2]
    cols = swap(pair_sends(first, last, "xline"), "xline", range(1, vintages), across)
    joined = lax.optimization_barrier((*got, *cols))
    got, cols = joined[:3], joined[3:]
    held = jnp.where(lax.axis_index("vintage") == 0, attr0, got[0] + got[1] + got[2])
    far = [lax.ppermute(held, "vintage", [(s, to[n]) for s, to in FANOUT.items()]) for n in (2, 1, 0)]
    semb, attr = attributes(tail_kernel, "tail", tile, *rows, *cols, *dips, semb0, attr0)
    correl = correlate(attr, held, far)
    return (semb[None], correl[None])


def solution(mesh):
    return jax.shard_map(
        per_device,
        mesh=mesh,
        in_specs=(
            P("vintage", "inline", "xline", None),
            P("vintage", "inline", "xline"),
            P("vintage", "inline", "xline"),
        ),
        out_specs=(P("vintage", "inline", "xline", None), P("vintage", "inline", "xline", None)),
        check_vma=False,
    )
```

```python
import jax
import jax.numpy as jnp
from jax import lax
from jax.experimental import pallas as pl
from jax.experimental.pallas import tpu as pltpu
from jax.sharding import PartitionSpec as P

TIME_SAMPLES = 256
MAX_DIP_STEP = 2
RT = 4
LAGS = 33
NWIN = 8
EPS = 1e-06

FANOUT = {0: (3, 2, 1), 4: (7, 6, 5), 8: (11, 10, 9), 12: (15, 14, 13)}
ROWS = 8
COLS = 16
TRACES = ROWS * COLS
PAD = 16
STEPS = (-1, 0, 1)


def steered(ref, lead, row, count, sign, dip):
    out = ref[lead, pl.ds(row, count), :]
    for k in range(-MAX_DIP_STEP, MAX_DIP_STEP + 1):
        if k:
            out = jnp.where(dip == k, ref[lead, pl.ds(row + sign * k, count), :], out)
    return out


def head_kernel(tile, row_12, row_23, row_01, cols, dip_il, dip_xl, *rest):
    @pl.when(lax.axis_index("vintage") == 0)
    def _():
        edges = cols[0:ROWS + 2], cols[ROWS + 2:]
        attr_body(tile, row_12, row_23, row_01, edges, dip_il, dip_xl, *rest)


def tail_kernel(tile, row_12, row_23, row_01, col_a, col_b, dip_il, dip_xl, semb_head, attr_head,
                semb_out, attr_out, *scratch):
    head = lax.axis_index("vintage") == 0

    @pl.when(head)
    def _():
        semb_out[...] = semb_head[...]
        attr_out[...] = attr_head[...]

    @pl.when(jnp.logical_not(head))
    def _():
        odd = lax.rem(lax.axis_index("xline"), 2) == 1
        edges = jnp.where(odd, col_a[...], col_b[...]), jnp.where(odd, col_b[...], col_a[...])
        attr_body(tile, row_12, row_23, row_01, edges, dip_il, dip_xl, semb_out, attr_out, *scratch)


def attr_body(tile, row_12, row_23, row_01, edges, dip_il, dip_xl, semb_out, attr_out,
              rim, moved, inner, sums, three):
    odd_row = lax.rem(lax.axis_index("inline"), 2) == 1
    rim[1:ROWS + 1, 1:COLS + 1, :] = tile[...]
    row_a, row_b = row_01[0] + row_23[0], row_12[0]
    rim[0, 1:COLS + 1, :] = jnp.where(odd_row, row_a, row_b)
    rim[ROWS + 1, 1:COLS + 1, :] = jnp.where(odd_row, row_b, row_a)
    rim[:, 0:1, :] = edges[0]
    rim[:, COLS + 1:COLS + 2, :] = edges[1]
    zeros = jnp.zeros((PAD, TRACES), jnp.float32)
    for a in STEPS:
        for b in STEPS:
            n = 3 * (a + 1) + b + 1
            block = rim[1 + a:1 + a + ROWS, 1 + b:1 + b + COLS, :].reshape(TRACES, TIME_SAMPLES)
            moved[n, 0:PAD, :] = zeros
            moved[n, PAD + TIME_SAMPLES:, :] = zeros
            moved[n, PAD:PAD + TIME_SAMPLES, :] = block.T
    q = jnp.broadcast_to(dip_xl[...], (8, TRACES))
    p = jnp.broadcast_to(dip_il[...], (8, TRACES))
    for r in range(0, TIME_SAMPLES + 16, 8):
        for a in STEPS:
            n = 3 * (a + 1) + 1
            mid = moved[n, pl.ds(r + 8, 8), :]
            lo = steered(moved, n - 1, r + 8, 8, -1, q)
            hi = steered(moved, n + 1, r + 8, 8, 1, q)
            inner[2 * (a + 1), pl.ds(r, 8), :] = lo + mid + hi
            inner[2 * (a + 1) + 1, pl.ds(r, 8), :] = lo * lo + mid * mid + hi * hi
    for r in range(0, TIME_SAMPLES + 8, 8):
        total = []
        for part in (0, 1):
            total.append(
                inner[2 + part, pl.ds(r + 4, 8), :]
                + steered(inner, part, r + 4, 8, -1, p)
                + steered(inner, 4 + part, r + 4, 8, 1, p)
            )
        sums[0, pl.ds(r, 8), :] = total[0]
        sums[1, pl.ds(r, 8), :] = total[0] * total[0]
        sums[2, pl.ds(r, 8), :] = total[1]
    for r in range(0, TIME_SAMPLES, 8):
        numer = sums[1, pl.ds(r, 8), :]
        denom = sums[2, pl.ds(r, 8), :]
        for s in range(1, 2 * RT + 1):
            numer = numer + sums[1, pl.ds(r + s, 8), :]
            denom = denom + sums[2, pl.ds(r + s, 8), :]
        semb = numer / (9.0 * denom + EPS)
        three[pl.ds(r, 8), :] = semb
        attr_out[pl.ds(r, 8), :] = semb * sums[0, pl.ds(r + RT, 8), :] * (1.0 / 9.0)
    semb_out[...] = three[...].T.reshape(ROWS, COLS, TIME_SAMPLES)


def pair_sum(x, y, half, low):
    return jnp.where(low, x, pltpu.roll(y, half, 0)) + jnp.where(low, pltpu.roll(x, 8 - half, 0), y)


def correl_kernel(mon, held, far3, far2, far1, out, base, result):
    half_lags = LAGS // 2
    holder = lax.rem(lax.axis_index("vintage"), 4) == 0
    zeros = jnp.zeros((half_lags, TRACES), jnp.float32)
    base[0:half_lags, :] = zeros
    base[half_lags + TIME_SAMPLES:, :] = zeros

    @pl.when(holder)
    def _():
        base[half_lags:half_lags + TIME_SAMPLES, :] = held[...]

    @pl.when(jnp.logical_not(holder))
    def _():
        base[half_lags:half_lags + TIME_SAMPLES, :] = far1[...] + far2[...] + far3[...]

    mon_energy = jnp.zeros((8, TRACES), jnp.float32)
    base_energy = jnp.zeros((8, TRACES), jnp.float32)
    for r in range(0, TIME_SAMPLES, 8):
        m = mon[pl.ds(r, 8), :]
        b = base[pl.ds(half_lags + r, 8), :]
        mon_energy = mon_energy + m * m
        base_energy = base_energy + b * b
    mon_energy = jnp.sum(mon_energy, axis=0, keepdims=True)
    base_energy = jnp.sum(base_energy, axis=0, keepdims=True)
    factor = NWIN / jnp.sqrt(mon_energy * base_energy + EPS)
    sub = lax.broadcasted_iota(jnp.int32, (8, TRACES), 0)
    width = TIME_SAMPLES // NWIN
    for lag in range(LAGS):
        level = []
        for w in range(NWIN):
            acc = None
            for r in range(w * width, (w + 1) * width, 8):
                term = mon[pl.ds(r, 8), :] * base[pl.ds(r + lag, 8), :]
                acc = term if acc is None else acc + term
            level.append(acc)
        level = [pair_sum(level[w], level[w + 4], 4, sub < 4) for w in range(4)]
        level = [pair_sum(level[w], level[w + 2], 2, (sub & 2) == 0) for w in range(2)]
        row = pair_sum(level[0], level[1], 1, (sub & 1) == 0)
        result[pl.ds(lag * 8, 8), :] = row * factor
    out[...] = result[...].T.reshape(ROWS, COLS, LAGS * NWIN)


def vmem(n):
    return [pl.BlockSpec(memory_space=pltpu.VMEM)] * n


def attributes(kernel, name, *args):
    return pl.pallas_call(
        kernel,
        out_shape=(
            jax.ShapeDtypeStruct((ROWS, COLS, TIME_SAMPLES), jnp.float32),
            jax.ShapeDtypeStruct((TIME_SAMPLES, TRACES), jnp.float32),
        ),
        in_specs=vmem(len(args)),
        out_specs=tuple(vmem(2)),
        scratch_shapes=[
            pltpu.VMEM((ROWS + 2, COLS + 8, TIME_SAMPLES), jnp.float32),
            pltpu.VMEM((9, TIME_SAMPLES + 2 * PAD, TRACES), jnp.float32),
            pltpu.VMEM((6, TIME_SAMPLES + 16, TRACES), jnp.float32),
            pltpu.VMEM((3, TIME_SAMPLES + 8, TRACES), jnp.float32),
            pltpu.VMEM((TIME_SAMPLES, TRACES), jnp.float32),
        ],
        compiler_params=pltpu.CompilerParams(vmem_limit_bytes=16 << 20),
        name=name,
    )(*args)


def correlate(mon, held, far):
    return pl.pallas_call(
        correl_kernel,
        out_shape=jax.ShapeDtypeStruct((ROWS, COLS, LAGS * NWIN), jnp.float32),
        in_specs=vmem(5),
        out_specs=pl.BlockSpec(memory_space=pltpu.VMEM),
        scratch_shapes=[
            pltpu.VMEM((TIME_SAMPLES + LAGS - 1, TRACES), jnp.float32),
            pltpu.VMEM((LAGS * NWIN, TRACES), jnp.float32),
        ],
        compiler_params=pltpu.CompilerParams(vmem_limit_bytes=16 << 20),
        name="correlate",
    )(mon, held, *far)


def pair_sends(first, last, axis):
    odd = lax.rem(lax.axis_index(axis), 2) == 1
    return jnp.where(odd, first, last), jnp.where(odd, last, first)


def swap(sends, axis, planes, rounds):
    count = lax.axis_size(axis)
    out = []
    for n, starts in enumerate(rounds):
        low = [(v * count + i, v * count + i + 1) for v in planes for i in starts]
        out.append(lax.ppermute(sends[n], ("vintage", axis), low + [(b, a) for a, b in low]))
    return out


def edge_columns(ends, rows):
    odd = lax.rem(lax.axis_index("inline"), 2) == 1
    row_a, row_b = rows[0] + rows[2], rows[1]
    above, below = jnp.where(odd, row_a, row_b), jnp.where(odd, row_b, row_a)
    return [
        jnp.concatenate([above[:, j:j + 1], end, below[:, j:j + 1]], axis=0)
        for j, end in zip((0, COLS - 1), ends)
    ]


def per_device(amplitude, inline_slope, crossline_slope):
    tile = amplitude[0]
    dips = (inline_slope.reshape(1, TRACES), crossline_slope.reshape(1, TRACES))
    vintages, width = lax.axis_size("vintage"), lax.axis_size("xline")
    along, across = ((0,), (1,), (2,)), ((0, 2, 4, 6), (1, 3, 5))
    sends = pair_sends(tile[:1], tile[-1:], "inline")
    outer = jnp.where(lax.axis_index("inline") == lax.axis_size("inline") - 1, tile[:1], tile[-1:])
    rows = swap((*sends, outer), "inline", range(vintages), along)
    first, last = edge_columns((tile[:, :1], tile[:, -1:]), rows)
    rows = [rows[n] for n in (1, 2, 0)]
    both = "vintage", "xline"
    left = lax.ppermute(last, both, [(x, width + x + 1) for x in range(width - 1)])
    right = lax.ppermute(first, both, [(x + 1, width + x) for x in range(width - 1)])
    cols = lax.ppermute(jnp.concatenate([left, right], axis=0), "vintage", [(1, 0)])
    semb0, attr0 = attributes(head_kernel, "head", tile, *rows, cols, *dips)
    got = [lax.ppermute(attr0, "vintage", [(0, k)]) for k in (12, 4, 8)]
    first, last = lax.optimization_barrier((first, last, attr0))[:2]
    cols = swap(pair_sends(first, last, "xline"), "xline", range(1, vintages), across)
    *got, col_b = lax.optimization_barrier((*got, cols[1]))
    cols = cols[0], col_b
    held = jnp.where(lax.axis_index("vintage") == 0, attr0, got[0] + got[1] + got[2])
    far = [lax.ppermute(held, "vintage", [(s, to[n]) for s, to in FANOUT.items()]) for n in (2, 1, 0)]
    semb, attr = attributes(tail_kernel, "tail", tile, *rows, *cols, *dips, semb0, attr0)
    correl = correlate(attr, held, far)
    return (semb[None], correl[None])


def solution(mesh):
    return jax.shard_map(
        per_device,
        mesh=mesh,
        in_specs=(
            P("vintage", "inline", "xline", None),
            P("vintage", "inline", "xline"),
            P("vintage", "inline", "xline"),
        ),
        out_specs=(P("vintage", "inline", "xline", None), P("vintage", "inline", "xline", None)),
        check_vma=False,
    )
```

```python
import jax
import jax.numpy as jnp
from jax import lax
from jax.experimental import pallas as pl
from jax.experimental.pallas import tpu as pltpu
from jax.sharding import PartitionSpec as P

TIME_SAMPLES = 256
MAX_DIP_STEP = 2
RT = 4
LAGS = 33
NWIN = 8
EPS = 1e-06

FANOUT = {0: (3, 2, 1), 4: (7, 6, 5), 8: (11, 10, 9), 12: (15, 14, 13)}
ROWS = 8
COLS = 16
TRACES = ROWS * COLS
PAD = 16
STEPS = (-1, 0, 1)


def steered(ref, lead, row, count, sign, dip):
    out = ref[lead, pl.ds(row, count), :]
    for k in range(-MAX_DIP_STEP, MAX_DIP_STEP + 1):
        if k:
            out = jnp.where(dip == k, ref[lead, pl.ds(row + sign * k, count), :], out)
    return out


def head_kernel(tile, row_12, row_23, row_01, cols, dip_il, dip_xl, *rest):
    @pl.when(lax.axis_index("vintage") == 0)
    def _():
        edges = cols[0:ROWS + 2], cols[ROWS + 2:]
        attr_body(tile, row_12, row_23, row_01, edges, dip_il, dip_xl, *rest)


def tail_kernel(tile, row_12, row_23, row_01, col_a, col_b, dip_il, dip_xl, semb_head, attr_head,
                semb_out, attr_out, *scratch):
    head = lax.axis_index("vintage") == 0

    @pl.when(head)
    def _():
        semb_out[...] = semb_head[...]
        attr_out[...] = attr_head[...]

    @pl.when(jnp.logical_not(head))
    def _():
        odd = lax.rem(lax.axis_index("xline"), 2) == 1
        edges = jnp.where(odd, col_a[...], col_b[...]), jnp.where(odd, col_b[...], col_a[...])
        attr_body(tile, row_12, row_23, row_01, edges, dip_il, dip_xl, semb_out, attr_out, *scratch)


def attr_body(tile, row_12, row_23, row_01, edges, dip_il, dip_xl, semb_out, attr_out,
              rim, moved, inner, sums, three):
    odd_row = lax.rem(lax.axis_index("inline"), 2) == 1
    rim[1:ROWS + 1, 1:COLS + 1, :] = tile[...]
    row_a, row_b = row_01[0] + row_23[0], row_12[0]
    rim[0, 1:COLS + 1, :] = jnp.where(odd_row, row_a, row_b)
    rim[ROWS + 1, 1:COLS + 1, :] = jnp.where(odd_row, row_b, row_a)
    rim[:, 0:1, :] = edges[0]
    rim[:, COLS + 1:COLS + 2, :] = edges[1]
    zeros = jnp.zeros((PAD, TRACES), jnp.float32)
    for a in STEPS:
        for b in STEPS:
            n = 3 * (a + 1) + b + 1
            block = rim[1 + a:1 + a + ROWS, 1 + b:1 + b + COLS, :].reshape(TRACES, TIME_SAMPLES)
            moved[n, 0:PAD, :] = zeros
            moved[n, PAD + TIME_SAMPLES:, :] = zeros
            moved[n, PAD:PAD + TIME_SAMPLES, :] = block.T
    q = jnp.broadcast_to(dip_xl[...], (8, TRACES))
    p = jnp.broadcast_to(dip_il[...], (8, TRACES))
    for r in range(0, TIME_SAMPLES + 16, 8):
        for a in STEPS:
            n = 3 * (a + 1) + 1
            mid = moved[n, pl.ds(r + 8, 8), :]
            lo = steered(moved, n - 1, r + 8, 8, -1, q)
            hi = steered(moved, n + 1, r + 8, 8, 1, q)
            inner[2 * (a + 1), pl.ds(r, 8), :] = lo + mid + hi
            inner[2 * (a + 1) + 1, pl.ds(r, 8), :] = lo * lo + mid * mid + hi * hi
    for r in range(0, TIME_SAMPLES + 8, 8):
        total = []
        for part in (0, 1):
            total.append(
                inner[2 + part, pl.ds(r + 4, 8), :]
                + steered(inner, part, r + 4, 8, -1, p)
                + steered(inner, 4 + part, r + 4, 8, 1, p)
            )
        sums[0, pl.ds(r, 8), :] = total[0]
        sums[1, pl.ds(r, 8), :] = total[0] * total[0]
        sums[2, pl.ds(r, 8), :] = total[1]
    for r in range(0, TIME_SAMPLES, 8):
        numer = sums[1, pl.ds(r, 8), :]
        denom = sums[2, pl.ds(r, 8), :]
        for s in range(1, 2 * RT + 1):
            numer = numer + sums[1, pl.ds(r + s, 8), :]
            denom = denom + sums[2, pl.ds(r + s, 8), :]
        semb = numer / (9.0 * denom + EPS)
        three[pl.ds(r, 8), :] = semb
        attr_out[pl.ds(r, 8), :] = semb * sums[0, pl.ds(r + RT, 8), :] * (1.0 / 9.0)
    semb_out[...] = three[...].T.reshape(ROWS, COLS, TIME_SAMPLES)


def pair_sum(x, y, half, low):
    return jnp.where(low, x, pltpu.roll(y, half, 0)) + jnp.where(low, pltpu.roll(x, 8 - half, 0), y)


def correl_kernel(mon, held, far3, far2, far1, out, base, result):
    half_lags = LAGS // 2
    holder = lax.rem(lax.axis_index("vintage"), 4) == 0
    zeros = jnp.zeros((half_lags, TRACES), jnp.float32)
    base[0:half_lags, :] = zeros
    base[half_lags + TIME_SAMPLES:, :] = zeros

    @pl.when(holder)
    def _():
        base[half_lags:half_lags + TIME_SAMPLES, :] = held[...]

    @pl.when(jnp.logical_not(holder))
    def _():
        base[half_lags:half_lags + TIME_SAMPLES, :] = far1[...] + far2[...] + far3[...]

    mon_energy = jnp.zeros((8, TRACES), jnp.float32)
    base_energy = jnp.zeros((8, TRACES), jnp.float32)
    for r in range(0, TIME_SAMPLES, 8):
        m = mon[pl.ds(r, 8), :]
        b = base[pl.ds(half_lags + r, 8), :]
        mon_energy = mon_energy + m * m
        base_energy = base_energy + b * b
    mon_energy = jnp.sum(mon_energy, axis=0, keepdims=True)
    base_energy = jnp.sum(base_energy, axis=0, keepdims=True)
    factor = NWIN / jnp.sqrt(mon_energy * base_energy + EPS)
    sub = lax.broadcasted_iota(jnp.int32, (8, TRACES), 0)
    width = TIME_SAMPLES // NWIN
    for lag in range(LAGS):
        level = []
        for w in range(NWIN):
            acc = None
            for r in range(w * width, (w + 1) * width, 8):
                term = mon[pl.ds(r, 8), :] * base[pl.ds(r + lag, 8), :]
                acc = term if acc is None else acc + term
            level.append(acc)
        level = [pair_sum(level[w], level[w + 4], 4, sub < 4) for w in range(4)]
        level = [pair_sum(level[w], level[w + 2], 2, (sub & 2) == 0) for w in range(2)]
        row = pair_sum(level[0], level[1], 1, (sub & 1) == 0)
        result[pl.ds(lag * 8, 8), :] = row * factor
    out[...] = result[...].T.reshape(ROWS, COLS, LAGS * NWIN)


def vmem(n):
    return [pl.BlockSpec(memory_space=pltpu.VMEM)] * n


def attributes(kernel, name, *args):
    return pl.pallas_call(
        kernel,
        out_shape=(
            jax.ShapeDtypeStruct((ROWS, COLS, TIME_SAMPLES), jnp.float32),
            jax.ShapeDtypeStruct((TIME_SAMPLES, TRACES), jnp.float32),
        ),
        in_specs=vmem(len(args)),
        out_specs=tuple(vmem(2)),
        scratch_shapes=[
            pltpu.VMEM((ROWS + 2, COLS + 8, TIME_SAMPLES), jnp.float32),
            pltpu.VMEM((9, TIME_SAMPLES + 2 * PAD, TRACES), jnp.float32),
            pltpu.VMEM((6, TIME_SAMPLES + 16, TRACES), jnp.float32),
            pltpu.VMEM((3, TIME_SAMPLES + 8, TRACES), jnp.float32),
            pltpu.VMEM((TIME_SAMPLES, TRACES), jnp.float32),
        ],
        compiler_params=pltpu.CompilerParams(vmem_limit_bytes=16 << 20),
        name=name,
    )(*args)


def correlate(mon, held, far):
    return pl.pallas_call(
        correl_kernel,
        out_shape=jax.ShapeDtypeStruct((ROWS, COLS, LAGS * NWIN), jnp.float32),
        in_specs=vmem(5),
        out_specs=pl.BlockSpec(memory_space=pltpu.VMEM),
        scratch_shapes=[
            pltpu.VMEM((TIME_SAMPLES + LAGS - 1, TRACES), jnp.float32),
            pltpu.VMEM((LAGS * NWIN, TRACES), jnp.float32),
        ],
        compiler_params=pltpu.CompilerParams(vmem_limit_bytes=16 << 20),
        name="correlate",
    )(mon, held, *far)


def pair_sends(first, last, axis):
    odd = lax.rem(lax.axis_index(axis), 2) == 1
    return jnp.where(odd, first, last), jnp.where(odd, last, first)


def swap(sends, axis, planes, rounds):
    count = lax.axis_size(axis)
    out = []
    for n, starts in enumerate(rounds):
        low = [(v * count + i, v * count + i + 1) for v in planes for i in starts]
        out.append(lax.ppermute(sends[n], ("vintage", axis), low + [(b, a) for a, b in low]))
    return out


def edge_columns(ends, rows):
    odd = lax.rem(lax.axis_index("inline"), 2) == 1
    row_a, row_b = rows[0] + rows[2], rows[1]
    above, below = jnp.where(odd, row_a, row_b), jnp.where(odd, row_b, row_a)
    return [
        jnp.concatenate([above[:, j:j + 1], end, below[:, j:j + 1]], axis=0)
        for j, end in zip((0, COLS - 1), ends)
    ]


def per_device(amplitude, inline_slope, crossline_slope):
    tile = amplitude[0]
    dips = (inline_slope.reshape(1, TRACES), crossline_slope.reshape(1, TRACES))
    vintages, width = lax.axis_size("vintage"), lax.axis_size("xline")
    along, across = ((0,), (1,), (2,)), ((0, 2, 4, 6), (1, 3, 5))
    sends = pair_sends(tile[:1], tile[-1:], "inline")
    outer = jnp.where(lax.axis_index("inline") == lax.axis_size("inline") - 1, tile[:1], tile[-1:])
    rows = swap((*sends, outer), "inline", range(vintages), along)
    first, last = edge_columns((tile[:, :1], tile[:, -1:]), rows)
    rows = [rows[n] for n in (1, 2, 0)]
    both = "vintage", "xline"
    left = lax.ppermute(last, both, [(x, width + x + 1) for x in range(width - 1)])
    right = lax.ppermute(first, both, [(x + 1, width + x) for x in range(width - 1)])
    cols = lax.ppermute(jnp.concatenate([left, right], axis=0), "vintage", [(1, 0)])
    semb0, attr0 = attributes(head_kernel, "head", tile, *rows, cols, *dips)
    got = [lax.ppermute(attr0, "vintage", [(0, k)]) for k in (8, 4, 12)]
    first, last = lax.optimization_barrier((first, last, attr0))[:2]
    cols = swap(pair_sends(first, last, "xline"), "xline", range(1, vintages), across)
    joined = lax.optimization_barrier((*got, *cols))
    got, cols = joined[:3], joined[3:]
    held = jnp.where(lax.axis_index("vintage") == 0, attr0, got[0] + got[1] + got[2])
    far = [lax.ppermute(held, "vintage", [(s, to[n]) for s, to in FANOUT.items()]) for n in (2, 1, 0)]
    semb, attr = attributes(tail_kernel, "tail", tile, *rows, *cols, *dips, semb0, attr0)
    correl = correlate(attr, held, far)
    return (semb[None], correl[None])


def solution(mesh):
    return jax.shard_map(
        per_device,
        mesh=mesh,
        in_specs=(
            P("vintage", "inline", "xline", None),
            P("vintage", "inline", "xline"),
            P("vintage", "inline", "xline"),
        ),
        out_specs=(P("vintage", "inline", "xline", None), P("vintage", "inline", "xline", None)),
        check_vma=False,
    )
```

```python
import jax
import jax.numpy as jnp
from jax import lax
from jax.experimental import pallas as pl
from jax.experimental.pallas import tpu as pltpu
from jax.sharding import PartitionSpec as P

TIME_SAMPLES = 256
MAX_DIP_STEP = 2
RT = 4
LAGS = 33
NWIN = 8
EPS = 1e-06

FANOUT = {0: (3, 2, 1), 4: (7, 6, 5), 8: (11, 10, 9), 12: (15, 14, 13)}
ROWS = 8
COLS = 16
TRACES = ROWS * COLS
PAD = 16
STEPS = (-1, 0, 1)


def steered(ref, lead, row, count, sign, dip):
    out = ref[lead, pl.ds(row, count), :]
    for k in range(-MAX_DIP_STEP, MAX_DIP_STEP + 1):
        if k:
            out = jnp.where(dip == k, ref[lead, pl.ds(row + sign * k, count), :], out)
    return out


def head_kernel(tile, row_12, row_23, row_01, cols, dip_il, dip_xl, *rest):
    @pl.when(lax.axis_index("vintage") == 0)
    def _():
        edges = cols[0:ROWS + 2], cols[ROWS + 2:]
        attr_body(tile, row_12, row_23, row_01, edges, dip_il, dip_xl, *rest)


def tail_kernel(tile, row_12, row_23, row_01, col_a, col_b, dip_il, dip_xl, semb_head, attr_head,
                semb_out, attr_out, *scratch):
    head = lax.axis_index("vintage") == 0

    @pl.when(head)
    def _():
        semb_out[...] = semb_head[...]
        attr_out[...] = attr_head[...]

    @pl.when(jnp.logical_not(head))
    def _():
        odd = lax.rem(lax.axis_index("xline"), 2) == 1
        edges = jnp.where(odd, col_a[...], col_b[...]), jnp.where(odd, col_b[...], col_a[...])
        attr_body(tile, row_12, row_23, row_01, edges, dip_il, dip_xl, semb_out, attr_out, *scratch)


def attr_body(tile, row_12, row_23, row_01, edges, dip_il, dip_xl, semb_out, attr_out,
              rim, moved, inner, sums, three):
    odd_row = lax.rem(lax.axis_index("inline"), 2) == 1
    rim[1:ROWS + 1, 1:COLS + 1, :] = tile[...]
    row_a, row_b = row_01[0] + row_23[0], row_12[0]
    rim[0, 1:COLS + 1, :] = jnp.where(odd_row, row_a, row_b)
    rim[ROWS + 1, 1:COLS + 1, :] = jnp.where(odd_row, row_b, row_a)
    rim[:, 0:1, :] = edges[0]
    rim[:, COLS + 1:COLS + 2, :] = edges[1]
    zeros = jnp.zeros((PAD, TRACES), jnp.float32)
    for a in STEPS:
        for b in STEPS:
            n = 3 * (a + 1) + b + 1
            block = rim[1 + a:1 + a + ROWS, 1 + b:1 + b + COLS, :].reshape(TRACES, TIME_SAMPLES)
            moved[n, 0:PAD, :] = zeros
            moved[n, PAD + TIME_SAMPLES:, :] = zeros
            moved[n, PAD:PAD + TIME_SAMPLES, :] = block.T
    q = jnp.broadcast_to(dip_xl[...], (8, TRACES))
    p = jnp.broadcast_to(dip_il[...], (8, TRACES))
    for r in range(0, TIME_SAMPLES + 16, 8):
        for a in STEPS:
            n = 3 * (a + 1) + 1
            mid = moved[n, pl.ds(r + 8, 8), :]
            lo = steered(moved, n - 1, r + 8, 8, -1, q)
            hi = steered(moved, n + 1, r + 8, 8, 1, q)
            inner[2 * (a + 1), pl.ds(r, 8), :] = lo + mid + hi
            inner[2 * (a + 1) + 1, pl.ds(r, 8), :] = lo * lo + mid * mid + hi * hi
    for r in range(0, TIME_SAMPLES + 8, 8):
        total = []
        for part in (0, 1):
            total.append(
                inner[2 + part, pl.ds(r + 4, 8), :]
                + steered(inner, part, r + 4, 8, -1, p)
                + steered(inner, 4 + part, r + 4, 8, 1, p)
            )
        sums[0, pl.ds(r, 8), :] = total[0]
        sums[1, pl.ds(r, 8), :] = total[0] * total[0]
        sums[2, pl.ds(r, 8), :] = total[1]
    for r in range(0, TIME_SAMPLES, 8):
        numer = sums[1, pl.ds(r, 8), :]
        denom = sums[2, pl.ds(r, 8), :]
        for s in range(1, 2 * RT + 1):
            numer = numer + sums[1, pl.ds(r + s, 8), :]
            denom = denom + sums[2, pl.ds(r + s, 8), :]
        semb = numer / (9.0 * denom + EPS)
        three[pl.ds(r, 8), :] = semb
        attr_out[pl.ds(r, 8), :] = semb * sums[0, pl.ds(r + RT, 8), :] * (1.0 / 9.0)
    semb_out[...] = three[...].T.reshape(ROWS, COLS, TIME_SAMPLES)


def pair_sum(x, y, half, low):
    return jnp.where(low, x, pltpu.roll(y, half, 0)) + jnp.where(low, pltpu.roll(x, 8 - half, 0), y)


def correl_kernel(mon, held, far3, far2, far1, out, base, result):
    half_lags = LAGS // 2
    holder = lax.rem(lax.axis_index("vintage"), 4) == 0
    zeros = jnp.zeros((half_lags, TRACES), jnp.float32)
    base[0:half_lags, :] = zeros
    base[half_lags + TIME_SAMPLES:, :] = zeros

    @pl.when(holder)
    def _():
        base[half_lags:half_lags + TIME_SAMPLES, :] = held[...]

    @pl.when(jnp.logical_not(holder))
    def _():
        base[half_lags:half_lags + TIME_SAMPLES, :] = far1[...] + far2[...] + far3[...]

    mon_energy = jnp.zeros((8, TRACES), jnp.float32)
    base_energy = jnp.zeros((8, TRACES), jnp.float32)
    for r in range(0, TIME_SAMPLES, 8):
        m = mon[pl.ds(r, 8), :]
        b = base[pl.ds(half_lags + r, 8), :]
        mon_energy = mon_energy + m * m
        base_energy = base_energy + b * b
    mon_energy = jnp.sum(mon_energy, axis=0, keepdims=True)
    base_energy = jnp.sum(base_energy, axis=0, keepdims=True)
    factor = NWIN / jnp.sqrt(mon_energy * base_energy + EPS)
    sub = lax.broadcasted_iota(jnp.int32, (8, TRACES), 0)
    width = TIME_SAMPLES // NWIN
    for lag in range(LAGS):
        level = []
        for w in range(NWIN):
            acc = None
            for r in range(w * width, (w + 1) * width, 8):
                term = mon[pl.ds(r, 8), :] * base[pl.ds(r + lag, 8), :]
                acc = term if acc is None else acc + term
            level.append(acc)
        level = [pair_sum(level[w], level[w + 4], 4, sub < 4) for w in range(4)]
        level = [pair_sum(level[w], level[w + 2], 2, (sub & 2) == 0) for w in range(2)]
        row = pair_sum(level[0], level[1], 1, (sub & 1) == 0)
        result[pl.ds(lag * 8, 8), :] = row * factor
    out[...] = result[...].T.reshape(ROWS, COLS, LAGS * NWIN)


def vmem(n):
    return [pl.BlockSpec(memory_space=pltpu.VMEM)] * n


def attributes(kernel, name, *args):
    return pl.pallas_call(
        kernel,
        out_shape=(
            jax.ShapeDtypeStruct((ROWS, COLS, TIME_SAMPLES), jnp.float32),
            jax.ShapeDtypeStruct((TIME_SAMPLES, TRACES), jnp.float32),
        ),
        in_specs=vmem(len(args)),
        out_specs=tuple(vmem(2)),
        scratch_shapes=[
            pltpu.VMEM((ROWS + 2, COLS + 8, TIME_SAMPLES), jnp.float32),
            pltpu.VMEM((9, TIME_SAMPLES + 2 * PAD, TRACES), jnp.float32),
            pltpu.VMEM((6, TIME_SAMPLES + 16, TRACES), jnp.float32),
            pltpu.VMEM((3, TIME_SAMPLES + 8, TRACES), jnp.float32),
            pltpu.VMEM((TIME_SAMPLES, TRACES), jnp.float32),
        ],
        compiler_params=pltpu.CompilerParams(vmem_limit_bytes=16 << 20),
        name=name,
    )(*args)


def correlate(mon, held, far):
    return pl.pallas_call(
        correl_kernel,
        out_shape=jax.ShapeDtypeStruct((ROWS, COLS, LAGS * NWIN), jnp.float32),
        in_specs=vmem(5),
        out_specs=pl.BlockSpec(memory_space=pltpu.VMEM),
        scratch_shapes=[
            pltpu.VMEM((TIME_SAMPLES + LAGS - 1, TRACES), jnp.float32),
            pltpu.VMEM((LAGS * NWIN, TRACES), jnp.float32),
        ],
        compiler_params=pltpu.CompilerParams(vmem_limit_bytes=16 << 20),
        name="correlate",
    )(mon, held, *far)


def pair_sends(first, last, axis):
    odd = lax.rem(lax.axis_index(axis), 2) == 1
    return jnp.where(odd, first, last), jnp.where(odd, last, first)


def swap(sends, axis, planes, rounds):
    count = lax.axis_size(axis)
    out = []
    for n, starts in enumerate(rounds):
        low = [(v * count + i, v * count + i + 1) for v in planes for i in starts]
        out.append(lax.ppermute(sends[n], ("vintage", axis), low + [(b, a) for a, b in low]))
    return out


def edge_columns(ends, rows):
    odd = lax.rem(lax.axis_index("inline"), 2) == 1
    row_a, row_b = rows[0] + rows[2], rows[1]
    above, below = jnp.where(odd, row_a, row_b), jnp.where(odd, row_b, row_a)
    return [
        jnp.concatenate([above[:, j:j + 1], end, below[:, j:j + 1]], axis=0)
        for j, end in zip((0, COLS - 1), ends)
    ]


def per_device(amplitude, inline_slope, crossline_slope):
    tile = amplitude[0]
    dips = (inline_slope.reshape(1, TRACES), crossline_slope.reshape(1, TRACES))
    vintages, width = lax.axis_size("vintage"), lax.axis_size("xline")
    along, across = ((0,), (1,), (2,)), ((0, 2, 4, 6), (1, 3, 5))
    sends = pair_sends(tile[:1], tile[-1:], "inline")
    outer = jnp.where(lax.axis_index("inline") == lax.axis_size("inline") - 1, tile[:1], tile[-1:])
    rows = swap((*sends, outer), "inline", range(vintages), along)
    first, last = edge_columns((tile[:, :1], tile[:, -1:]), rows)
    rows = [rows[n] for n in (1, 2, 0)]
    both = "vintage", "xline"
    left = lax.ppermute(last, both, [(x, width + x + 1) for x in range(width - 1)])
    right = lax.ppermute(first, both, [(x + 1, width + x) for x in range(width - 1)])
    cols = lax.ppermute(jnp.concatenate([left, right], axis=0), "vintage", [(1, 0)])
    semb0, attr0 = attributes(head_kernel, "head", tile, *rows, cols, *dips)
    got = [lax.ppermute(attr0, "vintage", [(0, k)]) for k in (4, 12, 8)]
    first, last = lax.optimization_barrier((first, last, attr0))[:2]
    cols = swap(pair_sends(first, last, "xline"), "xline", range(1, vintages), across)
    joined = lax.optimization_barrier((*got, *cols))
    got, cols = joined[:3], joined[3:]
    held = jnp.where(lax.axis_index("vintage") == 0, attr0, got[0] + got[1] + got[2])
    far = [lax.ppermute(held, "vintage", [(s, to[n]) for s, to in FANOUT.items()]) for n in (2, 1, 0)]
    semb, attr = attributes(tail_kernel, "tail", tile, *rows, *cols, *dips, semb0, attr0)
    correl = correlate(attr, held, far)
    return (semb[None], correl[None])


def solution(mesh):
    return jax.shard_map(
        per_device,
        mesh=mesh,
        in_specs=(
            P("vintage", "inline", "xline", None),
            P("vintage", "inline", "xline"),
            P("vintage", "inline", "xline"),
        ),
        out_specs=(P("vintage", "inline", "xline", None), P("vintage", "inline", "xline", None)),
        check_vma=False,
    )
```

```python
import jax
import jax.numpy as jnp
from jax import lax
from jax.experimental import pallas as pl
from jax.experimental.pallas import tpu as pltpu
from jax.sharding import PartitionSpec as P

TIME_SAMPLES = 256
MAX_DIP_STEP = 2
RT = 4
LAGS = 33
NWIN = 8
EPS = 1e-06

FANOUT = {0: (3, 2, 1), 4: (7, 6, 5), 8: (11, 10, 9), 12: (15, 14, 13)}
ROWS = 8
COLS = 16
TRACES = ROWS * COLS
PAD = 16
STEPS = (-1, 0, 1)


def steered(ref, lead, row, count, sign, dip):
    out = ref[lead, pl.ds(row, count), :]
    for k in range(-MAX_DIP_STEP, MAX_DIP_STEP + 1):
        if k:
            out = jnp.where(dip == k, ref[lead, pl.ds(row + sign * k, count), :], out)
    return out


def head_kernel(tile, row_12, row_23, row_01, cols, dip_il, dip_xl, *rest):
    @pl.when(lax.axis_index("vintage") == 0)
    def _():
        edges = cols[0:ROWS + 2], cols[ROWS + 2:]
        attr_body(tile, row_12, row_23, row_01, edges, dip_il, dip_xl, *rest)


def tail_kernel(tile, row_12, row_23, row_01, col_a, col_b, dip_il, dip_xl, semb_head, attr_head,
                semb_out, attr_out, *scratch):
    head = lax.axis_index("vintage") == 0

    @pl.when(head)
    def _():
        semb_out[...] = semb_head[...]
        attr_out[...] = attr_head[...]

    @pl.when(jnp.logical_not(head))
    def _():
        odd = lax.rem(lax.axis_index("xline"), 2) == 1
        edges = jnp.where(odd, col_a[...], col_b[...]), jnp.where(odd, col_b[...], col_a[...])
        attr_body(tile, row_12, row_23, row_01, edges, dip_il, dip_xl, semb_out, attr_out, *scratch)


def attr_body(tile, row_12, row_23, row_01, edges, dip_il, dip_xl, semb_out, attr_out,
              rim, moved, inner, sums, three):
    odd_row = lax.rem(lax.axis_index("inline"), 2) == 1
    rim[1:ROWS + 1, 1:COLS + 1, :] = tile[...]
    row_a, row_b = row_01[0] + row_23[0], row_12[0]
    rim[0, 1:COLS + 1, :] = jnp.where(odd_row, row_a, row_b)
    rim[ROWS + 1, 1:COLS + 1, :] = jnp.where(odd_row, row_b, row_a)
    rim[:, 0:1, :] = edges[0]
    rim[:, COLS + 1:COLS + 2, :] = edges[1]
    zeros = jnp.zeros((PAD, TRACES), jnp.float32)
    for a in STEPS:
        for b in STEPS:
            n = 3 * (a + 1) + b + 1
            block = rim[1 + a:1 + a + ROWS, 1 + b:1 + b + COLS, :].reshape(TRACES, TIME_SAMPLES)
            moved[n, 0:PAD, :] = zeros
            moved[n, PAD + TIME_SAMPLES:, :] = zeros
            moved[n, PAD:PAD + TIME_SAMPLES, :] = block.T
    q = jnp.broadcast_to(dip_xl[...], (8, TRACES))
    p = jnp.broadcast_to(dip_il[...], (8, TRACES))
    for r in range(0, TIME_SAMPLES + 16, 8):
        for a in STEPS:
            n = 3 * (a + 1) + 1
            mid = moved[n, pl.ds(r + 8, 8), :]
            lo = steered(moved, n - 1, r + 8, 8, -1, q)
            hi = steered(moved, n + 1, r + 8, 8, 1, q)
            inner[2 * (a + 1), pl.ds(r, 8), :] = lo + mid + hi
            inner[2 * (a + 1) + 1, pl.ds(r, 8), :] = lo * lo + mid * mid + hi * hi
    for r in range(0, TIME_SAMPLES + 8, 8):
        total = []
        for part in (0, 1):
            total.append(
                inner[2 + part, pl.ds(r + 4, 8), :]
                + steered(inner, part, r + 4, 8, -1, p)
                + steered(inner, 4 + part, r + 4, 8, 1, p)
            )
        sums[0, pl.ds(r, 8), :] = total[0]
        sums[1, pl.ds(r, 8), :] = total[0] * total[0]
        sums[2, pl.ds(r, 8), :] = total[1]
    for r in range(0, TIME_SAMPLES, 8):
        numer = sums[1, pl.ds(r, 8), :]
        denom = sums[2, pl.ds(r, 8), :]
        for s in range(1, 2 * RT + 1):
            numer = numer + sums[1, pl.ds(r + s, 8), :]
            denom = denom + sums[2, pl.ds(r + s, 8), :]
        semb = numer / (9.0 * denom + EPS)
        three[pl.ds(r, 8), :] = semb
        attr_out[pl.ds(r, 8), :] = semb * sums[0, pl.ds(r + RT, 8), :] * (1.0 / 9.0)
    semb_out[...] = three[...].T.reshape(ROWS, COLS, TIME_SAMPLES)


def pair_sum(x, y, half, low):
    return jnp.where(low, x, pltpu.roll(y, half, 0)) + jnp.where(low, pltpu.roll(x, 8 - half, 0), y)


def correl_kernel(mon, held, far3, far2, far1, out, base, result):
    half_lags = LAGS // 2
    holder = lax.rem(lax.axis_index("vintage"), 4) == 0
    zeros = jnp.zeros((half_lags, TRACES), jnp.float32)
    base[0:half_lags, :] = zeros
    base[half_lags + TIME_SAMPLES:, :] = zeros

    @pl.when(holder)
    def _():
        base[half_lags:half_lags + TIME_SAMPLES, :] = held[...]

    @pl.when(jnp.logical_not(holder))
    def _():
        base[half_lags:half_lags + TIME_SAMPLES, :] = far1[...] + far2[...] + far3[...]

    mon_energy = jnp.zeros((8, TRACES), jnp.float32)
    base_energy = jnp.zeros((8, TRACES), jnp.float32)
    for r in range(0, TIME_SAMPLES, 8):
        m = mon[pl.ds(r, 8), :]
        b = base[pl.ds(half_lags + r, 8), :]
        mon_energy = mon_energy + m * m
        base_energy = base_energy + b * b
    mon_energy = jnp.sum(mon_energy, axis=0, keepdims=True)
    base_energy = jnp.sum(base_energy, axis=0, keepdims=True)
    factor = NWIN / jnp.sqrt(mon_energy * base_energy + EPS)
    sub = lax.broadcasted_iota(jnp.int32, (8, TRACES), 0)
    width = TIME_SAMPLES // NWIN
    for lag in range(LAGS):
        level = []
        for w in range(NWIN):
            acc = None
            for r in range(w * width, (w + 1) * width, 8):
                term = mon[pl.ds(r, 8), :] * base[pl.ds(r + lag, 8), :]
                acc = term if acc is None else acc + term
            level.append(acc)
        level = [pair_sum(level[w], level[w + 4], 4, sub < 4) for w in range(4)]
        level = [pair_sum(level[w], level[w + 2], 2, (sub & 2) == 0) for w in range(2)]
        row = pair_sum(level[0], level[1], 1, (sub & 1) == 0)
        result[pl.ds(lag * 8, 8), :] = row * factor
    out[...] = result[...].T.reshape(ROWS, COLS, LAGS * NWIN)


def vmem(n):
    return [pl.BlockSpec(memory_space=pltpu.VMEM)] * n


def attributes(kernel, name, *args):
    return pl.pallas_call(
        kernel,
        out_shape=(
            jax.ShapeDtypeStruct((ROWS, COLS, TIME_SAMPLES), jnp.float32),
            jax.ShapeDtypeStruct((TIME_SAMPLES, TRACES), jnp.float32),
        ),
        in_specs=vmem(len(args)),
        out_specs=tuple(vmem(2)),
        scratch_shapes=[
            pltpu.VMEM((ROWS + 2, COLS + 8, TIME_SAMPLES), jnp.float32),
            pltpu.VMEM((9, TIME_SAMPLES + 2 * PAD, TRACES), jnp.float32),
            pltpu.VMEM((6, TIME_SAMPLES + 16, TRACES), jnp.float32),
            pltpu.VMEM((3, TIME_SAMPLES + 8, TRACES), jnp.float32),
            pltpu.VMEM((TIME_SAMPLES, TRACES), jnp.float32),
        ],
        compiler_params=pltpu.CompilerParams(vmem_limit_bytes=16 << 20),
        name=name,
    )(*args)


def correlate(mon, held, far):
    return pl.pallas_call(
        correl_kernel,
        out_shape=jax.ShapeDtypeStruct((ROWS, COLS, LAGS * NWIN), jnp.float32),
        in_specs=vmem(5),
        out_specs=pl.BlockSpec(memory_space=pltpu.VMEM),
        scratch_shapes=[
            pltpu.VMEM((TIME_SAMPLES + LAGS - 1, TRACES), jnp.float32),
            pltpu.VMEM((LAGS * NWIN, TRACES), jnp.float32),
        ],
        compiler_params=pltpu.CompilerParams(vmem_limit_bytes=16 << 20),
        name="correlate",
    )(mon, held, *far)


def pair_sends(first, last, axis):
    odd = lax.rem(lax.axis_index(axis), 2) == 1
    return jnp.where(odd, first, last), jnp.where(odd, last, first)


def swap(sends, axis, planes, rounds):
    count = lax.axis_size(axis)
    out = []
    for n, starts in enumerate(rounds):
        low = [(v * count + i, v * count + i + 1) for v in planes for i in starts]
        out.append(lax.ppermute(sends[n], ("vintage", axis), low + [(b, a) for a, b in low]))
    return out


def edge_columns(ends, rows):
    odd = lax.rem(lax.axis_index("inline"), 2) == 1
    row_a, row_b = rows[0] + rows[2], rows[1]
    above, below = jnp.where(odd, row_a, row_b), jnp.where(odd, row_b, row_a)
    return [
        jnp.concatenate([above[:, j:j + 1], end, below[:, j:j + 1]], axis=0)
        for j, end in zip((0, COLS - 1), ends)
    ]


def per_device(amplitude, inline_slope, crossline_slope):
    tile = amplitude[0]
    dips = (inline_slope.reshape(1, TRACES), crossline_slope.reshape(1, TRACES))
    vintages, width = lax.axis_size("vintage"), lax.axis_size("xline")
    along, across = ((0,), (1,), (2,)), ((0, 2, 4, 6), (1, 3, 5))
    sends = pair_sends(tile[:1], tile[-1:], "inline")
    outer = jnp.where(lax.axis_index("inline") == lax.axis_size("inline") - 1, tile[:1], tile[-1:])
    rows = swap((*sends, outer), "inline", range(vintages), along)
    first, last = edge_columns((tile[:, :1], tile[:, -1:]), rows)
    rows = [rows[n] for n in (1, 2, 0)]
    both = "vintage", "xline"
    left = lax.ppermute(last, both, [(x, width + x + 1) for x in range(width - 1)])
    right = lax.ppermute(first, both, [(x + 1, width + x) for x in range(width - 1)])
    cols = lax.ppermute(jnp.concatenate([left, right], axis=0), "vintage", [(1, 0)])
    semb0, attr0 = attributes(head_kernel, "head", tile, *rows, cols, *dips)
    got = [lax.ppermute(attr0, "vintage", [(0, k)]) for k in (4, 12, 8)]
    first, last = lax.optimization_barrier((first, last, attr0))[:2]
    cols = swap(pair_sends(first, last, "xline"), "xline", range(1, vintages), across)
    joined = lax.optimization_barrier((*cols[::-1], *got))
    got, cols = joined[2:], joined[1::-1]
    held = jnp.where(lax.axis_index("vintage") == 0, attr0, got[0] + got[1] + got[2])
    far = [lax.ppermute(held, "vintage", [(s, to[n]) for s, to in FANOUT.items()]) for n in (2, 1, 0)]
    semb, attr = attributes(tail_kernel, "tail", tile, *rows, *cols, *dips, semb0, attr0)
    correl = correlate(attr, held, far)
    return (semb[None], correl[None])


def solution(mesh):
    return jax.shard_map(
        per_device,
        mesh=mesh,
        in_specs=(
            P("vintage", "inline", "xline", None),
            P("vintage", "inline", "xline"),
            P("vintage", "inline", "xline"),
        ),
        out_specs=(P("vintage", "inline", "xline", None), P("vintage", "inline", "xline", None)),
        check_vma=False,
    )
```

```python
import functools

import jax
import jax.numpy as jnp
from jax import lax
from jax.experimental import pallas as pl
from jax.experimental.pallas import tpu as pltpu
from jax.sharding import PartitionSpec as P

TIME_SAMPLES = 256
MAX_DIP_STEP = 2
RT = 4
LAGS = 33
NWIN = 8
EPS = 1e-06

FANOUT = {0: (3, 2, 1), 4: (7, 6, 5), 8: (11, 10, 9), 12: (15, 14, 13)}
ROWS = 8
COLS = 16
TRACES = ROWS * COLS
PAD = 16
STEPS = (-1, 0, 1)


def steered(ref, lead, row, count, sign, dip):
    out = ref[lead, pl.ds(row, count), :]
    for k in range(-MAX_DIP_STEP, MAX_DIP_STEP + 1):
        if k:
            out = jnp.where(dip == k, ref[lead, pl.ds(row + sign * k, count), :], out)
    return out


def head_kernel(tile, row_12, row_23, row_01, cols, dip_il, dip_xl, *rest):
    @pl.when(lax.axis_index("vintage") == 0)
    def _():
        edges = cols[0:ROWS + 2], cols[ROWS + 2:]
        attr_body(tile, row_12, row_23, row_01, edges, dip_il, dip_xl, *rest)


def tail_kernel(tile, row_12, row_23, row_01, col_a, col_b, dip_il, dip_xl, semb_head, attr_head,
                semb_out, attr_out, *scratch):
    head = lax.axis_index("vintage") == 0

    @pl.when(head)
    def _():
        semb_out[...] = semb_head[...]
        attr_out[...] = attr_head[...]

    @pl.when(jnp.logical_not(head))
    def _():
        odd = lax.rem(lax.axis_index("xline"), 2) == 1
        edges = jnp.where(odd, col_a[...], col_b[...]), jnp.where(odd, col_b[...], col_a[...])
        attr_body(tile, row_12, row_23, row_01, edges, dip_il, dip_xl, semb_out, attr_out, *scratch)


def attr_body(tile, row_12, row_23, row_01, edges, dip_il, dip_xl, semb_out, attr_out,
              rim, moved, inner, sums, three):
    odd_row = lax.rem(lax.axis_index("inline"), 2) == 1
    rim[1:ROWS + 1, 1:COLS + 1, :] = tile[...]
    row_a, row_b = row_01[0] + row_23[0], row_12[0]
    rim[0, 1:COLS + 1, :] = jnp.where(odd_row, row_a, row_b)
    rim[ROWS + 1, 1:COLS + 1, :] = jnp.where(odd_row, row_b, row_a)
    rim[:, 0:1, :] = edges[0]
    rim[:, COLS + 1:COLS + 2, :] = edges[1]
    zeros = jnp.zeros((PAD, TRACES), jnp.float32)
    for a in STEPS:
        for b in STEPS:
            n = 3 * (a + 1) + b + 1
            block = rim[1 + a:1 + a + ROWS, 1 + b:1 + b + COLS, :].reshape(TRACES, TIME_SAMPLES)
            moved[n, 0:PAD, :] = zeros
            moved[n, PAD + TIME_SAMPLES:, :] = zeros
            moved[n, PAD:PAD + TIME_SAMPLES, :] = block.T
    q = jnp.broadcast_to(dip_xl[...], (8, TRACES))
    p = jnp.broadcast_to(dip_il[...], (8, TRACES))
    for r in range(0, TIME_SAMPLES + 16, 8):
        for a in STEPS:
            n = 3 * (a + 1) + 1
            mid = moved[n, pl.ds(r + 8, 8), :]
            lo = steered(moved, n - 1, r + 8, 8, -1, q)
            hi = steered(moved, n + 1, r + 8, 8, 1, q)
            inner[2 * (a + 1), pl.ds(r, 8), :] = lo + mid + hi
            inner[2 * (a + 1) + 1, pl.ds(r, 8), :] = lo * lo + mid * mid + hi * hi
    for r in range(0, TIME_SAMPLES + 8, 8):
        total = []
        for part in (0, 1):
            total.append(
                inner[2 + part, pl.ds(r + 4, 8), :]
                + steered(inner, part, r + 4, 8, -1, p)
                + steered(inner, 4 + part, r + 4, 8, 1, p)
            )
        sums[0, pl.ds(r, 8), :] = total[0]
        sums[1, pl.ds(r, 8), :] = total[0] * total[0]
        sums[2, pl.ds(r, 8), :] = total[1]
    for r in range(0, TIME_SAMPLES, 8):
        numer = sums[1, pl.ds(r, 8), :]
        denom = sums[2, pl.ds(r, 8), :]
        for s in range(1, 2 * RT + 1):
            numer = numer + sums[1, pl.ds(r + s, 8), :]
            denom = denom + sums[2, pl.ds(r + s, 8), :]
        semb = numer / (9.0 * denom + EPS)
        three[pl.ds(r, 8), :] = semb
        attr_out[pl.ds(r, 8), :] = semb * sums[0, pl.ds(r + RT, 8), :] * (1.0 / 9.0)
    semb_out[...] = three[...].T.reshape(ROWS, COLS, TIME_SAMPLES)


def pair_sum(x, y, half, low):
    return jnp.where(low, x, pltpu.roll(y, half, 0)) + jnp.where(low, pltpu.roll(x, 8 - half, 0), y)


def correl_kernel(mon, held, far3, far2, far1, out, base, result):
    half_lags = LAGS // 2
    holder = lax.rem(lax.axis_index("vintage"), 4) == 0
    zeros = jnp.zeros((half_lags, TRACES), jnp.float32)
    base[0:half_lags, :] = zeros
    base[half_lags + TIME_SAMPLES:, :] = zeros

    @pl.when(holder)
    def _():
        base[half_lags:half_lags + TIME_SAMPLES, :] = held[...]

    @pl.when(jnp.logical_not(holder))
    def _():
        base[half_lags:half_lags + TIME_SAMPLES, :] = far1[...] + far2[...] + far3[...]

    mon_energy = jnp.zeros((8, TRACES), jnp.float32)
    base_energy = jnp.zeros((8, TRACES), jnp.float32)
    for r in range(0, TIME_SAMPLES, 8):
        m = mon[pl.ds(r, 8), :]
        b = base[pl.ds(half_lags + r, 8), :]
        mon_energy = mon_energy + m * m
        base_energy = base_energy + b * b
    mon_energy = jnp.sum(mon_energy, axis=0, keepdims=True)
    base_energy = jnp.sum(base_energy, axis=0, keepdims=True)
    factor = NWIN / jnp.sqrt(mon_energy * base_energy + EPS)
    sub = lax.broadcasted_iota(jnp.int32, (8, TRACES), 0)
    width = TIME_SAMPLES // NWIN
    for first in range(8):
        lags = range(first, LAGS, 8)
        sums = [[] for _ in lags]
        for w in range(NWIN):
            row = w * width
            m = [mon[pl.ds(row + 8 * k, 8), :] for k in range(width // 8)]
            b = [base[pl.ds(row + first + 8 * k, 8), :] for k in range(width // 8 + len(lags) - 1)]
            for n, level in enumerate(sums):
                level.append(functools.reduce(jnp.add, [x * y for x, y in zip(m, b[n:])]))
        for lag, level in zip(lags, sums):
            level = [pair_sum(level[w], level[w + 4], 4, sub < 4) for w in range(4)]
            level = [pair_sum(level[w], level[w + 2], 2, (sub & 2) == 0) for w in range(2)]
            row = pair_sum(level[0], level[1], 1, (sub & 1) == 0)
            result[pl.ds(lag * 8, 8), :] = row * factor
    out[...] = result[...].T.reshape(ROWS, COLS, LAGS * NWIN)


def vmem(n):
    return [pl.BlockSpec(memory_space=pltpu.VMEM)] * n


def attributes(kernel, name, *args):
    return pl.pallas_call(
        kernel,
        out_shape=(
            jax.ShapeDtypeStruct((ROWS, COLS, TIME_SAMPLES), jnp.float32),
            jax.ShapeDtypeStruct((TIME_SAMPLES, TRACES), jnp.float32),
        ),
        in_specs=vmem(len(args)),
        out_specs=tuple(vmem(2)),
        scratch_shapes=[
            pltpu.VMEM((ROWS + 2, COLS + 8, TIME_SAMPLES), jnp.float32),
            pltpu.VMEM((9, TIME_SAMPLES + 2 * PAD, TRACES), jnp.float32),
            pltpu.VMEM((6, TIME_SAMPLES + 16, TRACES), jnp.float32),
            pltpu.VMEM((3, TIME_SAMPLES + 8, TRACES), jnp.float32),
            pltpu.VMEM((TIME_SAMPLES, TRACES), jnp.float32),
        ],
        compiler_params=pltpu.CompilerParams(vmem_limit_bytes=16 << 20),
        name=name,
    )(*args)


def correlate(mon, held, far):
    return pl.pallas_call(
        correl_kernel,
        out_shape=jax.ShapeDtypeStruct((ROWS, COLS, LAGS * NWIN), jnp.float32),
        in_specs=vmem(5),
        out_specs=pl.BlockSpec(memory_space=pltpu.VMEM),
        scratch_shapes=[
            pltpu.VMEM((TIME_SAMPLES + LAGS - 1, TRACES), jnp.float32),
            pltpu.VMEM((LAGS * NWIN, TRACES), jnp.float32),
        ],
        compiler_params=pltpu.CompilerParams(vmem_limit_bytes=16 << 20),
        name="correlate",
    )(mon, held, *far)


def pair_sends(first, last, axis):
    odd = lax.rem(lax.axis_index(axis), 2) == 1
    return jnp.where(odd, first, last), jnp.where(odd, last, first)


def swap(sends, axis, planes, rounds):
    count = lax.axis_size(axis)
    out = []
    for n, starts in enumerate(rounds):
        low = [(v * count + i, v * count + i + 1) for v in planes for i in starts]
        out.append(lax.ppermute(sends[n], ("vintage", axis), low + [(b, a) for a, b in low]))
    return out


def edge_columns(ends, rows):
    odd = lax.rem(lax.axis_index("inline"), 2) == 1
    row_a, row_b = rows[0] + rows[2], rows[1]
    above, below = jnp.where(odd, row_a, row_b), jnp.where(odd, row_b, row_a)
    return [
        jnp.concatenate([above[:, j:j + 1], end, below[:, j:j + 1]], axis=0)
        for j, end in zip((0, COLS - 1), ends)
    ]


def per_device(amplitude, inline_slope, crossline_slope):
    tile = amplitude[0]
    dips = (inline_slope.reshape(1, TRACES), crossline_slope.reshape(1, TRACES))
    vintages, width = lax.axis_size("vintage"), lax.axis_size("xline")
    along, across = ((0,), (1,), (2,)), ((0, 2, 4, 6), (1, 3, 5))
    sends = pair_sends(tile[:1], tile[-1:], "inline")
    outer = jnp.where(lax.axis_index("inline") == lax.axis_size("inline") - 1, tile[:1], tile[-1:])
    rows = swap((*sends, outer), "inline", range(vintages), along)
    first, last = edge_columns((tile[:, :1], tile[:, -1:]), rows)
    rows = [rows[n] for n in (1, 2, 0)]
    both = "vintage", "xline"
    left = lax.ppermute(last, both, [(x, width + x + 1) for x in range(width - 1)])
    right = lax.ppermute(first, both, [(x + 1, width + x) for x in range(width - 1)])
    cols = lax.ppermute(jnp.concatenate([left, right], axis=0), "vintage", [(1, 0)])
    semb0, attr0 = attributes(head_kernel, "head", tile, *rows, cols, *dips)
    got = [lax.ppermute(attr0, "vintage", [(0, k)]) for k in (4, 12, 8)]
    first, last = lax.optimization_barrier((first, last, attr0))[:2]
    cols = swap(pair_sends(first, last, "xline"), "xline", range(1, vintages), across)
    joined = lax.optimization_barrier((*got, *cols))
    got, cols = joined[:3], joined[3:]
    held = jnp.where(lax.axis_index("vintage") == 0, attr0, got[0] + got[1] + got[2])
    far = [lax.ppermute(held, "vintage", [(s, to[n]) for s, to in FANOUT.items()]) for n in (2, 1, 0)]
    semb, attr = attributes(tail_kernel, "tail", tile, *rows, *cols, *dips, semb0, attr0)
    correl = correlate(attr, held, far)
    return (semb[None], correl[None])


def solution(mesh):
    return jax.shard_map(
        per_device,
        mesh=mesh,
        in_specs=(
            P("vintage", "inline", "xline", None),
            P("vintage", "inline", "xline"),
            P("vintage", "inline", "xline"),
        ),
        out_specs=(P("vintage", "inline", "xline", None), P("vintage", "inline", "xline", None)),
        check_vma=False,
    )
```

```python
import jax
import jax.numpy as jnp
from jax import lax
from jax.experimental import pallas as pl
from jax.experimental.pallas import tpu as pltpu
from jax.sharding import PartitionSpec as P

TIME_SAMPLES = 256
MAX_DIP_STEP = 2
RT = 4
LAGS = 33
NWIN = 8
EPS = 1e-06

FANOUT = {0: (3, 2, 1), 4: (7, 6, 5), 8: (11, 10, 9), 12: (15, 14, 13)}
ROWS = 8
COLS = 16
TRACES = ROWS * COLS
PAD = 16
STEPS = (-1, 0, 1)


def steered(ref, lead, row, count, sign, dip):
    out = ref[lead, pl.ds(row, count), :]
    for k in range(-MAX_DIP_STEP, MAX_DIP_STEP + 1):
        if k:
            out = jnp.where(dip == k, ref[lead, pl.ds(row + sign * k, count), :], out)
    return out


def head_kernel(tile, row_12, row_23, row_01, cols, dip_il, dip_xl, *rest):
    @pl.when(lax.axis_index("vintage") == 0)
    def _():
        edges = cols[0:ROWS + 2], cols[ROWS + 2:]
        attr_body(tile, row_12, row_23, row_01, edges, dip_il, dip_xl, *rest[:-1])


def tail_kernel(tile, row_12, row_23, row_01, col_a, col_b, dip_il, dip_xl, semb_head, attr_head,
                semb_out, attr_out, *scratch):
    head = lax.axis_index("vintage") == 0

    @pl.when(head)
    def _():
        semb_out[...] = semb_head[...].T.reshape(ROWS, COLS, TIME_SAMPLES)
        attr_out[...] = attr_head[...]

    @pl.when(jnp.logical_not(head))
    def _():
        odd = lax.rem(lax.axis_index("xline"), 2) == 1
        edges = jnp.where(odd, col_a[...], col_b[...]), jnp.where(odd, col_b[...], col_a[...])
        attr_body(tile, row_12, row_23, row_01, edges, dip_il, dip_xl, scratch[-1], attr_out, *scratch[:-1])
        semb_out[...] = scratch[-1][...].T.reshape(ROWS, COLS, TIME_SAMPLES)


def attr_body(tile, row_12, row_23, row_01, edges, dip_il, dip_xl, three, attr_out,
              rim, moved, inner, sums):
    odd_row = lax.rem(lax.axis_index("inline"), 2) == 1
    rim[1:ROWS + 1, 1:COLS + 1, :] = tile[...]
    row_a, row_b = row_01[0] + row_23[0], row_12[0]
    rim[0, 1:COLS + 1, :] = jnp.where(odd_row, row_a, row_b)
    rim[ROWS + 1, 1:COLS + 1, :] = jnp.where(odd_row, row_b, row_a)
    rim[:, 0:1, :] = edges[0]
    rim[:, COLS + 1:COLS + 2, :] = edges[1]
    zeros = jnp.zeros((PAD, TRACES), jnp.float32)
    for a in STEPS:
        for b in STEPS:
            n = 3 * (a + 1) + b + 1
            block = rim[1 + a:1 + a + ROWS, 1 + b:1 + b + COLS, :].reshape(TRACES, TIME_SAMPLES)
            moved[n, 0:PAD, :] = zeros
            moved[n, PAD + TIME_SAMPLES:, :] = zeros
            moved[n, PAD:PAD + TIME_SAMPLES, :] = block.T
    q = jnp.broadcast_to(dip_xl[...], (8, TRACES))
    p = jnp.broadcast_to(dip_il[...], (8, TRACES))
    for r in range(0, TIME_SAMPLES + 16, 8):
        for a in STEPS:
            n = 3 * (a + 1) + 1
            mid = moved[n, pl.ds(r + 8, 8), :]
            lo = steered(moved, n - 1, r + 8, 8, -1, q)
            hi = steered(moved, n + 1, r + 8, 8, 1, q)
            inner[2 * (a + 1), pl.ds(r, 8), :] = lo + mid + hi
            inner[2 * (a + 1) + 1, pl.ds(r, 8), :] = lo * lo + mid * mid + hi * hi
    for r in range(0, TIME_SAMPLES + 8, 8):
        total = []
        for part in (0, 1):
            total.append(
                inner[2 + part, pl.ds(r + 4, 8), :]
                + steered(inner, part, r + 4, 8, -1, p)
                + steered(inner, 4 + part, r + 4, 8, 1, p)
            )
        sums[0, pl.ds(r, 8), :] = total[0]
        sums[1, pl.ds(r, 8), :] = total[0] * total[0]
        sums[2, pl.ds(r, 8), :] = total[1]
    for r in range(0, TIME_SAMPLES, 8):
        numer = sums[1, pl.ds(r, 8), :]
        denom = sums[2, pl.ds(r, 8), :]
        for s in range(1, 2 * RT + 1):
            numer = numer + sums[1, pl.ds(r + s, 8), :]
            denom = denom + sums[2, pl.ds(r + s, 8), :]
        semb = numer / (9.0 * denom + EPS)
        three[pl.ds(r, 8), :] = semb
        attr_out[pl.ds(r, 8), :] = semb * sums[0, pl.ds(r + RT, 8), :] * (1.0 / 9.0)


def pair_sum(x, y, half, low):
    return jnp.where(low, x, pltpu.roll(y, half, 0)) + jnp.where(low, pltpu.roll(x, 8 - half, 0), y)


def correl_kernel(mon, held, far3, far2, far1, out, base, result):
    half_lags = LAGS // 2
    holder = lax.rem(lax.axis_index("vintage"), 4) == 0
    zeros = jnp.zeros((half_lags, TRACES), jnp.float32)
    base[0:half_lags, :] = zeros
    base[half_lags + TIME_SAMPLES:, :] = zeros

    @pl.when(holder)
    def _():
        base[half_lags:half_lags + TIME_SAMPLES, :] = held[...]

    @pl.when(jnp.logical_not(holder))
    def _():
        base[half_lags:half_lags + TIME_SAMPLES, :] = far1[...] + far2[...] + far3[...]

    mon_energy = jnp.zeros((8, TRACES), jnp.float32)
    base_energy = jnp.zeros((8, TRACES), jnp.float32)
    for r in range(0, TIME_SAMPLES, 8):
        m = mon[pl.ds(r, 8), :]
        b = base[pl.ds(half_lags + r, 8), :]
        mon_energy = mon_energy + m * m
        base_energy = base_energy + b * b
    mon_energy = jnp.sum(mon_energy, axis=0, keepdims=True)
    base_energy = jnp.sum(base_energy, axis=0, keepdims=True)
    factor = NWIN / jnp.sqrt(mon_energy * base_energy + EPS)
    sub = lax.broadcasted_iota(jnp.int32, (8, TRACES), 0)
    width = TIME_SAMPLES // NWIN
    for lag in range(LAGS):
        level = []
        for w in range(NWIN):
            acc = None
            for r in range(w * width, (w + 1) * width, 8):
                term = mon[pl.ds(r, 8), :] * base[pl.ds(r + lag, 8), :]
                acc = term if acc is None else acc + term
            level.append(acc)
        level = [pair_sum(level[w], level[w + 4], 4, sub < 4) for w in range(4)]
        level = [pair_sum(level[w], level[w + 2], 2, (sub & 2) == 0) for w in range(2)]
        row = pair_sum(level[0], level[1], 1, (sub & 1) == 0)
        result[pl.ds(lag * 8, 8), :] = row * factor
    out[...] = result[...].T.reshape(ROWS, COLS, LAGS * NWIN)


def vmem(n):
    return [pl.BlockSpec(memory_space=pltpu.VMEM)] * n


def attributes(kernel, name, semb_shape, *args):
    return pl.pallas_call(
        kernel,
        out_shape=(
            jax.ShapeDtypeStruct(semb_shape, jnp.float32),
            jax.ShapeDtypeStruct((TIME_SAMPLES, TRACES), jnp.float32),
        ),
        in_specs=vmem(len(args)),
        out_specs=tuple(vmem(2)),
        scratch_shapes=[
            pltpu.VMEM((ROWS + 2, COLS + 8, TIME_SAMPLES), jnp.float32),
            pltpu.VMEM((9, TIME_SAMPLES + 2 * PAD, TRACES), jnp.float32),
            pltpu.VMEM((6, TIME_SAMPLES + 16, TRACES), jnp.float32),
            pltpu.VMEM((3, TIME_SAMPLES + 8, TRACES), jnp.float32),
            pltpu.VMEM((TIME_SAMPLES, TRACES), jnp.float32),
        ],
        compiler_params=pltpu.CompilerParams(vmem_limit_bytes=16 << 20),
        name=name,
    )(*args)


def correlate(mon, held, far):
    return pl.pallas_call(
        correl_kernel,
        out_shape=jax.ShapeDtypeStruct((ROWS, COLS, LAGS * NWIN), jnp.float32),
        in_specs=vmem(5),
        out_specs=pl.BlockSpec(memory_space=pltpu.VMEM),
        scratch_shapes=[
            pltpu.VMEM((TIME_SAMPLES + LAGS - 1, TRACES), jnp.float32),
            pltpu.VMEM((LAGS * NWIN, TRACES), jnp.float32),
        ],
        compiler_params=pltpu.CompilerParams(vmem_limit_bytes=16 << 20),
        name="correlate",
    )(mon, held, *far)


def pair_sends(first, last, axis):
    odd = lax.rem(lax.axis_index(axis), 2) == 1
    return jnp.where(odd, first, last), jnp.where(odd, last, first)


def swap(sends, axis, planes, rounds):
    count = lax.axis_size(axis)
    out = []
    for n, starts in enumerate(rounds):
        low = [(v * count + i, v * count + i + 1) for v in planes for i in starts]
        out.append(lax.ppermute(sends[n], ("vintage", axis), low + [(b, a) for a, b in low]))
    return out


def edge_columns(ends, rows):
    odd = lax.rem(lax.axis_index("inline"), 2) == 1
    row_a, row_b = rows[0] + rows[2], rows[1]
    above, below = jnp.where(odd, row_a, row_b), jnp.where(odd, row_b, row_a)
    return [
        jnp.concatenate([above[:, j:j + 1], end, below[:, j:j + 1]], axis=0)
        for j, end in zip((0, COLS - 1), ends)
    ]


def per_device(amplitude, inline_slope, crossline_slope):
    tile = amplitude[0]
    dips = (inline_slope.reshape(1, TRACES), crossline_slope.reshape(1, TRACES))
    vintages, width = lax.axis_size("vintage"), lax.axis_size("xline")
    along, across = ((0,), (1,), (2,)), ((0, 2, 4, 6), (1, 3, 5))
    sends = pair_sends(tile[:1], tile[-1:], "inline")
    outer = jnp.where(lax.axis_index("inline") == lax.axis_size("inline") - 1, tile[:1], tile[-1:])
    rows = swap((*sends, outer), "inline", range(vintages), along)
    first, last = edge_columns((tile[:, :1], tile[:, -1:]), rows)
    rows = [rows[n] for n in (1, 2, 0)]
    both = "vintage", "xline"
    left = lax.ppermute(last, both, [(x, width + x + 1) for x in range(width - 1)])
    right = lax.ppermute(first, both, [(x + 1, width + x) for x in range(width - 1)])
    cols = lax.ppermute(jnp.concatenate([left, right], axis=0), "vintage", [(1, 0)])
    semb0, attr0 = attributes(head_kernel, "head", (TIME_SAMPLES, TRACES), tile, *rows, cols, *dips)
    got = [lax.ppermute(attr0, "vintage", [(0, k)]) for k in (4, 12, 8)]
    first, last = lax.optimization_barrier((first, last, attr0))[:2]
    cols = swap(pair_sends(first, last, "xline"), "xline", range(1, vintages), across)
    joined = lax.optimization_barrier((*got, *cols))
    got, cols = joined[:3], joined[3:]
    held = jnp.where(lax.axis_index("vintage") == 0, attr0, got[0] + got[1] + got[2])
    far = [lax.ppermute(held, "vintage", [(s, to[n]) for s, to in FANOUT.items()]) for n in (2, 1, 0)]
    semb, attr = attributes(tail_kernel, "tail", (ROWS, COLS, TIME_SAMPLES), tile, *rows, *cols, *dips, semb0, attr0)
    correl = correlate(attr, held, far)
    return (semb[None], correl[None])


def solution(mesh):
    return jax.shard_map(
        per_device,
        mesh=mesh,
        in_specs=(
            P("vintage", "inline", "xline", None),
            P("vintage", "inline", "xline"),
            P("vintage", "inline", "xline"),
        ),
        out_specs=(P("vintage", "inline", "xline", None), P("vintage", "inline", "xline", None)),
        check_vma=False,
    )
```

```python
import jax
import jax.numpy as jnp
from jax import lax
from jax.experimental import pallas as pl
from jax.experimental.pallas import tpu as pltpu
from jax.sharding import PartitionSpec as P

TIME_SAMPLES = 256
MAX_DIP_STEP = 2
RT = 4
LAGS = 33
NWIN = 8
EPS = 1e-06

FANOUT = {0: (2, 3, 1), 4: (6, 7, 5), 8: (10, 11, 9), 12: (14, 15, 13)}
ROWS = 8
COLS = 16
TRACES = ROWS * COLS
PAD = 16
STEPS = (-1, 0, 1)


def steered(ref, lead, row, count, sign, dip):
    out = ref[lead, pl.ds(row, count), :]
    for k in range(-MAX_DIP_STEP, MAX_DIP_STEP + 1):
        if k:
            out = jnp.where(dip == k, ref[lead, pl.ds(row + sign * k, count), :], out)
    return out


def head_kernel(tile, row_12, row_23, row_01, cols, dip_il, dip_xl, *rest):
    @pl.when(lax.axis_index("vintage") == 0)
    def _():
        edges = cols[0:ROWS + 2], cols[ROWS + 2:]
        attr_body(tile, row_12, row_23, row_01, edges, dip_il, dip_xl, *rest)


def tail_kernel(tile, row_12, row_23, row_01, col_a, col_b, dip_il, dip_xl, semb_head, attr_head,
                semb_out, attr_out, *scratch):
    head = lax.axis_index("vintage") == 0

    @pl.when(head)
    def _():
        semb_out[...] = semb_head[...]
        attr_out[...] = attr_head[...]

    @pl.when(jnp.logical_not(head))
    def _():
        odd = lax.rem(lax.axis_index("xline"), 2) == 1
        edges = jnp.where(odd, col_a[...], col_b[...]), jnp.where(odd, col_b[...], col_a[...])
        attr_body(tile, row_12, row_23, row_01, edges, dip_il, dip_xl, semb_out, attr_out, *scratch)


def attr_body(tile, row_12, row_23, row_01, edges, dip_il, dip_xl, semb_out, attr_out,
              rim, moved, inner, sums, three):
    odd_row = lax.rem(lax.axis_index("inline"), 2) == 1
    rim[1:ROWS + 1, 1:COLS + 1, :] = tile[...]
    row_a, row_b = row_01[0] + row_23[0], row_12[0]
    rim[0, 1:COLS + 1, :] = jnp.where(odd_row, row_a, row_b)
    rim[ROWS + 1, 1:COLS + 1, :] = jnp.where(odd_row, row_b, row_a)
    rim[:, 0:1, :] = edges[0]
    rim[:, COLS + 1:COLS + 2, :] = edges[1]
    zeros = jnp.zeros((PAD, TRACES), jnp.float32)
    for a in STEPS:
        for b in STEPS:
            n = 3 * (a + 1) + b + 1
            block = rim[1 + a:1 + a + ROWS, 1 + b:1 + b + COLS, :].reshape(TRACES, TIME_SAMPLES)
            moved[n, 0:PAD, :] = zeros
            moved[n, PAD + TIME_SAMPLES:, :] = zeros
            moved[n, PAD:PAD + TIME_SAMPLES, :] = block.T
    q = jnp.broadcast_to(dip_xl[...], (8, TRACES))
    p = jnp.broadcast_to(dip_il[...], (8, TRACES))
    for r in range(0, TIME_SAMPLES + 16, 8):
        for a in STEPS:
            n = 3 * (a + 1) + 1
            mid = moved[n, pl.ds(r + 8, 8), :]
            lo = steered(moved, n - 1, r + 8, 8, -1, q)
            hi = steered(moved, n + 1, r + 8, 8, 1, q)
            inner[2 * (a + 1), pl.ds(r, 8), :] = lo + mid + hi
            inner[2 * (a + 1) + 1, pl.ds(r, 8), :] = lo * lo + mid * mid + hi * hi
    for r in range(0, TIME_SAMPLES + 8, 8):
        total = []
        for part in (0, 1):
            total.append(
                inner[2 + part, pl.ds(r + 4, 8), :]
                + steered(inner, part, r + 4, 8, -1, p)
                + steered(inner, 4 + part, r + 4, 8, 1, p)
            )
        sums[0, pl.ds(r, 8), :] = total[0]
        sums[1, pl.ds(r, 8), :] = total[0] * total[0]
        sums[2, pl.ds(r, 8), :] = total[1]
    for r in range(0, TIME_SAMPLES, 8):
        numer = sums[1, pl.ds(r, 8), :]
        denom = sums[2, pl.ds(r, 8), :]
        for s in range(1, 2 * RT + 1):
            numer = numer + sums[1, pl.ds(r + s, 8), :]
            denom = denom + sums[2, pl.ds(r + s, 8), :]
        semb = numer / (9.0 * denom + EPS)
        three[pl.ds(r, 8), :] = semb
        attr_out[pl.ds(r, 8), :] = semb * sums[0, pl.ds(r + RT, 8), :] * (1.0 / 9.0)
    semb_out[...] = three[...].T.reshape(ROWS, COLS, TIME_SAMPLES)


def pair_sum(x, y, half, low):
    return jnp.where(low, x, pltpu.roll(y, half, 0)) + jnp.where(low, pltpu.roll(x, 8 - half, 0), y)


def correl_kernel(mon, held, far3, far2, far1, out, base, result):
    half_lags = LAGS // 2
    holder = lax.rem(lax.axis_index("vintage"), 4) == 0
    zeros = jnp.zeros((half_lags, TRACES), jnp.float32)
    base[0:half_lags, :] = zeros
    base[half_lags + TIME_SAMPLES:, :] = zeros

    @pl.when(holder)
    def _():
        base[half_lags:half_lags + TIME_SAMPLES, :] = held[...]

    @pl.when(jnp.logical_not(holder))
    def _():
        base[half_lags:half_lags + TIME_SAMPLES, :] = far1[...] + far2[...] + far3[...]

    mon_energy = jnp.zeros((8, TRACES), jnp.float32)
    base_energy = jnp.zeros((8, TRACES), jnp.float32)
    for r in range(0, TIME_SAMPLES, 8):
        m = mon[pl.ds(r, 8), :]
        b = base[pl.ds(half_lags + r, 8), :]
        mon_energy = mon_energy + m * m
        base_energy = base_energy + b * b
    mon_energy = jnp.sum(mon_energy, axis=0, keepdims=True)
    base_energy = jnp.sum(base_energy, axis=0, keepdims=True)
    factor = NWIN / jnp.sqrt(mon_energy * base_energy + EPS)
    sub = lax.broadcasted_iota(jnp.int32, (8, TRACES), 0)
    width = TIME_SAMPLES // NWIN
    for lag in range(LAGS):
        level = []
        for w in range(NWIN):
            acc = None
            for r in range(w * width, (w + 1) * width, 8):
                term = mon[pl.ds(r, 8), :] * base[pl.ds(r + lag, 8), :]
                acc = term if acc is None else acc + term
            level.append(acc)
        level = [pair_sum(level[w], level[w + 4], 4, sub < 4) for w in range(4)]
        level = [pair_sum(level[w], level[w + 2], 2, (sub & 2) == 0) for w in range(2)]
        row = pair_sum(level[0], level[1], 1, (sub & 1) == 0)
        result[pl.ds(lag * 8, 8), :] = row * factor
    out[...] = result[...].T.reshape(ROWS, COLS, LAGS * NWIN)


def vmem(n):
    return [pl.BlockSpec(memory_space=pltpu.VMEM)] * n


def attributes(kernel, name, *args):
    return pl.pallas_call(
        kernel,
        out_shape=(
            jax.ShapeDtypeStruct((ROWS, COLS, TIME_SAMPLES), jnp.float32),
            jax.ShapeDtypeStruct((TIME_SAMPLES, TRACES), jnp.float32),
        ),
        in_specs=vmem(len(args)),
        out_specs=tuple(vmem(2)),
        scratch_shapes=[
            pltpu.VMEM((ROWS + 2, COLS + 8, TIME_SAMPLES), jnp.float32),
            pltpu.VMEM((9, TIME_SAMPLES + 2 * PAD, TRACES), jnp.float32),
            pltpu.VMEM((6, TIME_SAMPLES + 16, TRACES), jnp.float32),
            pltpu.VMEM((3, TIME_SAMPLES + 8, TRACES), jnp.float32),
            pltpu.VMEM((TIME_SAMPLES, TRACES), jnp.float32),
        ],
        compiler_params=pltpu.CompilerParams(vmem_limit_bytes=16 << 20),
        name=name,
    )(*args)


def correlate(mon, held, far):
    return pl.pallas_call(
        correl_kernel,
        out_shape=jax.ShapeDtypeStruct((ROWS, COLS, LAGS * NWIN), jnp.float32),
        in_specs=vmem(5),
        out_specs=pl.BlockSpec(memory_space=pltpu.VMEM),
        scratch_shapes=[
            pltpu.VMEM((TIME_SAMPLES + LAGS - 1, TRACES), jnp.float32),
            pltpu.VMEM((LAGS * NWIN, TRACES), jnp.float32),
        ],
        compiler_params=pltpu.CompilerParams(vmem_limit_bytes=16 << 20),
        name="correlate",
    )(mon, held, *far)


def pair_sends(first, last, axis):
    odd = lax.rem(lax.axis_index(axis), 2) == 1
    return jnp.where(odd, first, last), jnp.where(odd, last, first)


def swap(sends, axis, planes, rounds):
    count = lax.axis_size(axis)
    out = []
    for n, starts in enumerate(rounds):
        low = [(v * count + i, v * count + i + 1) for v in planes for i in starts]
        out.append(lax.ppermute(sends[n], ("vintage", axis), low + [(b, a) for a, b in low]))
    return out


def edge_columns(ends, rows):
    odd = lax.rem(lax.axis_index("inline"), 2) == 1
    row_a, row_b = rows[0] + rows[2], rows[1]
    above, below = jnp.where(odd, row_a, row_b), jnp.where(odd, row_b, row_a)
    return [
        jnp.concatenate([above[:, j:j + 1], end, below[:, j:j + 1]], axis=0)
        for j, end in zip((0, COLS - 1), ends)
    ]


def per_device(amplitude, inline_slope, crossline_slope):
    tile = amplitude[0]
    dips = (inline_slope.reshape(1, TRACES), crossline_slope.reshape(1, TRACES))
    vintages, width = lax.axis_size("vintage"), lax.axis_size("xline")
    along, across = ((0,), (1,), (2,)), ((0, 2, 4, 6), (1, 3, 5))
    sends = pair_sends(tile[:1], tile[-1:], "inline")
    outer = jnp.where(lax.axis_index("inline") == lax.axis_size("inline") - 1, tile[:1], tile[-1:])
    rows = swap((*sends, outer), "inline", range(vintages), along)
    first, last = edge_columns((tile[:, :1], tile[:, -1:]), rows)
    rows = [rows[n] for n in (1, 2, 0)]
    both = "vintage", "xline"
    left = lax.ppermute(last, both, [(x, width + x + 1) for x in range(width - 1)])
    right = lax.ppermute(first, both, [(x + 1, width + x) for x in range(width - 1)])
    cols = lax.ppermute(jnp.concatenate([left, right], axis=0), "vintage", [(1, 0)])
    semb0, attr0 = attributes(head_kernel, "head", tile, *rows, cols, *dips)
    got = [lax.ppermute(attr0, "vintage", [(0, k)]) for k in (4, 12, 8)]
    first, last = lax.optimization_barrier((first, last, attr0))[:2]
    cols = swap(pair_sends(first, last, "xline"), "xline", range(1, vintages), across)
    joined = lax.optimization_barrier((*got, *cols))
    got, cols = joined[:3], joined[3:]
    held = jnp.where(lax.axis_index("vintage") == 0, attr0, got[0] + got[1] + got[2])
    far = [lax.ppermute(held, "vintage", [(s, to[n]) for s, to in FANOUT.items()]) for n in (2, 1, 0)]
    semb, attr = attributes(tail_kernel, "tail", tile, *rows, *cols, *dips, semb0, attr0)
    correl = correlate(attr, held, far)
    return (semb[None], correl[None])


def solution(mesh):
    return jax.shard_map(
        per_device,
        mesh=mesh,
        in_specs=(
            P("vintage", "inline", "xline", None),
            P("vintage", "inline", "xline"),
            P("vintage", "inline", "xline"),
        ),
        out_specs=(P("vintage", "inline", "xline", None), P("vintage", "inline", "xline", None)),
        check_vma=False,
    )
```
